256 devices in a mesh: seq: 16 (over z, core), rep: 16 (over x, y).
Axes of the slice: x: 4, y: 4, z: 8, core: 2. Of those that a mesh axis runs over, the one named last changes fastest.
Arguments:
- tokens: bfloat16 [65536, 1024], P(('rep', 'seq')), parts along dimension 0, may hold values from -16 to 16
- segments: int32 [65536], P(('rep', 'seq')), parts along dimension 0, may hold values from 0 to 3, never falling along the last dimension, each value on 1 to 2048 neighbouring positions
- qkv_weight: bfloat16 [1024, 3072], replicated, may hold values from -1 to 1
- out_weight: bfloat16 [1024, 1024], replicated, may hold values from -0.1875 to 0.1875
- out_bias: float32 [1024], replicated, may hold values from -3 to 3
- ln_gain: float32 [1024], replicated, may hold values from 0.1 to 1.9
- ln_bias: float32 [1024], replicated, may hold values from -3 to 3
Outputs:
- normed: bfloat16 [65536, 1024], P(('rep', 'seq')), parts along dimension 0
- kv_cache: bfloat16 [65536, 2048], P('rep', 'seq'), parts along dimension 0
The draws below stay inside these ranges and needn't reach their ends.
There are 16 independent parts, one for each index of `rep`. The reference program is written for one: setup_inputs(seed, part) draws one part's arguments, and reference() takes and returns one part's arrays. A program takes and returns all parts, laid end to end along the dimension named above; an argument that names none is the same for every part. Nothing has to cross between parts.
Inputs may be any that keep to these rules, and one draw needn't show every extreme that they name: `segments`: each prompt is a contiguous run of 1 to 2048 tokens, numbers never falling, one prompt exactly 2048 tokens.
All inputs are finite; a program needn't handle non-finite values.
Results may differ from the reference program's by a relative error of at most 0.008.
Values may be sent and summed in bfloat16 or wider, within the bound.
A program may use at most 128 MiB of HBM per device.

```python
import math
import jax
import jax.numpy as jnp
import numpy as np
from jax import lax

HEADS = 16
HEAD = 64
D = 1024
TOKENS = 4096
SEGS = 4
SEG_MOST = 2048


def draw_tokens(key, part):
    keys = jax.random.split(jax.random.fold_in(key, 11), 2)
    result = jnp.clip(jax.random.normal(keys[1], (TOKENS, D)), -6.0, 6.0)
    return result.astype(jnp.bfloat16)


def draw_qkv_weight(key, part):
    keys = jax.random.split(jax.random.fold_in(key, 23), 1)
    base = jax.random.normal(keys[0], (D, HEADS, 3, HEAD)) * D ** (-0.5)
    base = jnp.clip(base, -0.9, 0.9)
    return base.reshape(D, 3 * D).astype(jnp.bfloat16)


def profile(amount, total, most, slope):
    weights = [(1 << 20) // math.isqrt(grade ** slope) + 1 for grade in range(2, amount + 1)]
    surplus, holding = total - most - (amount - 1), [1] * (amount - 1)
    while surplus > 0:
        candidates = [i for i in range(amount - 1) if holding[i] < most]
        whole, budget = sum([weights[i] for i in candidates]), surplus
        for i in candidates:
            more = min(most - holding[i], max(1, budget * weights[i] // whole), surplus)
            holding[i] = holding[i] + more
            surplus = surplus - more
    return np.array([most] + holding)


def ragged_sizes(stream_key, amount, total, limit, skew):
    if amount == 2:
        one = jax.random.randint(stream_key, (), max(1, total - limit), min(limit, total - 1) + 1)
        return jnp.stack([one, total - one])
    sizes = jnp.asarray(profile(amount, total, limit, skew), jnp.int32)
    couples = (amount - 1) // 2
    source_of, taker = sizes[1:1 + 2 * couples:2], sizes[2:2 + 2 * couples:2]
    room = jnp.minimum(source_of - 1, limit - taker)
    moved = jax.random.randint(jax.random.fold_in(stream_key, 1), (couples,), 0, 1 << 20) % (room + 1)
    sizes = sizes.at[1:1 + 2 * couples:2].set(source_of - moved).at[2:2 + 2 * couples:2].set(taker + moved)
    return sizes[jax.random.permutation(jax.random.fold_in(stream_key, 2), amount)]


def centred(key, dims, spread, reach, kind=jnp.bfloat16):
    array = spread * jax.random.normal(key, dims, jnp.float32)
    return jnp.clip(array, min=-reach, max=reach).astype(kind)


def setup_inputs(seed: int = 0, part: int = 0) -> dict:
    streams_of = jax.random.split(jax.random.key(seed), 8)
    part_keys = jax.random.split(jax.random.fold_in(streams_of[7], part), 8)
    tokens = draw_tokens(jax.random.fold_in(jax.random.fold_in(streams_of[7], part), 71), part)
    segments = jnp.searchsorted(jnp.cumsum(ragged_sizes(part_keys[1], SEGS, TOKENS, SEG_MOST, 2)), jnp.arange(TOKENS), side="right").astype(jnp.int32)
    qkv_weight = draw_qkv_weight(jax.random.fold_in(streams_of[7], 71), part)
    out_weight = centred(streams_of[3], (D, D), D ** -0.5, 0.1875)
    out_bias = centred(streams_of[4], (D,), 0.5, 3.0, jnp.float32)
    ln_gain = jnp.clip(1.0 + 0.18 * jax.random.normal(streams_of[5], (D,), jnp.float32), 0.1, 1.9)
    ln_bias = centred(streams_of[6], (D,), 0.5, 3.0, jnp.float32)
    return dict(tokens=tokens, segments=segments, qkv_weight=qkv_weight, out_weight=out_weight, out_bias=out_bias, ln_gain=ln_gain, ln_bias=ln_bias)


def reference(tokens, segments, qkv_weight, out_weight, out_bias, ln_gain, ln_bias):
    proj = jnp.dot(tokens, qkv_weight, preferred_element_type=jnp.float32).astype(jnp.bfloat16)
    grouped = proj.reshape(TOKENS, HEADS, 3, HEAD)
    kv_cache = grouped[:, :, 1:, :].reshape(TOKENS, 2 * D)
    per_head = jnp.moveaxis(grouped, 1, 0)
    same = segments[:, None] == segments[None, :]
    scale = 1.0 / HEAD ** 0.5

    def one_head(block):
        query = block[:, 0, :]
        keys = block[:, 1, :]
        values = block[:, 2, :]
        score = jnp.dot(query, keys.T, preferred_element_type=jnp.float32) * scale
        score = jnp.where(same, score, -jnp.inf)
        top = lax.optimization_barrier(jnp.max(score, axis=1, keepdims=True))
        weight = jnp.where(same, jnp.exp(score - top), 0.0)
        total = lax.optimization_barrier(jnp.sum(weight, axis=1, keepdims=True))
        context = jnp.dot(weight.astype(jnp.bfloat16), values, preferred_element_type=jnp.float32) / total
        return context.astype(jnp.bfloat16)
    context = lax.map(one_head, per_head)
    context = jnp.moveaxis(context, 0, 1).reshape(TOKENS, D)
    mixed = jnp.dot(context, out_weight, preferred_element_type=jnp.float32) + out_bias + tokens.astype(jnp.float32)
    mean = lax.optimization_barrier(jnp.mean(mixed, axis=1, keepdims=True))
    centered = mixed - mean
    variance = lax.optimization_barrier(jnp.mean(centered * centered, axis=1, keepdims=True))
    normed = centered / jnp.sqrt(variance + 1e-05) * ln_gain + ln_bias
    return (normed.astype(jnp.bfloat16), kv_cache)
```

```python
import math

import jax
import jax.numpy as jnp
from jax import lax
from jax.sharding import PartitionSpec as P

HEADS = 16
HEAD = 64
Q_CHUNK = 512


def shards(tokens, segments, qkv_weight, out_weight, out_bias, ln_gain, ln_bias):
    tok_rows, width = tokens.shape
    scale = 1.0 / math.sqrt(HEAD)
    all_seg = lax.all_gather(segments, "seq", axis=0, tiled=True)
    proj = jnp.dot(tokens, qkv_weight, preferred_element_type=jnp.float32).astype(jnp.bfloat16)
    grouped = proj.reshape(tok_rows, HEADS, 3 * HEAD)
    mine = lax.all_to_all(grouped, "seq", split_axis=1, concat_axis=0, tiled=True)
    count_rows = mine.shape[0]
    mine = mine.reshape(count_rows, 3 * HEAD)
    kv_cache = mine[:, HEAD:]
    query = mine[:, :HEAD]
    key_h = mine[:, HEAD:2 * HEAD]
    value_h = mine[:, 2 * HEAD:]
    chunks = count_rows // Q_CHUNK

    def per_chunk(items):
        q_c, seg_c = items
        kept = seg_c[:, None] == all_seg[None, :]
        score = jnp.dot(q_c, key_h.T, preferred_element_type=jnp.float32) * scale
        score = jnp.where(kept, score, -1e30)
        top = jnp.max(score, axis=1, keepdims=True)
        weight = jnp.where(kept, jnp.exp(score - top), 0.0)
        total = jnp.sum(weight, axis=1, keepdims=True)
        acc = jnp.dot(weight.astype(jnp.bfloat16), value_h, preferred_element_type=jnp.float32)
        return (acc / total).astype(jnp.bfloat16)

    context = lax.map(
        per_chunk,
        (query.reshape(chunks, Q_CHUNK, HEAD), all_seg.reshape(chunks, Q_CHUNK)),
    ).reshape(count_rows, 1, HEAD)
    gathered_ctx = lax.all_to_all(context, "seq", split_axis=0, concat_axis=1, tiled=True)
    gathered_ctx = gathered_ctx.reshape(tok_rows, width)
    mixed = (
        jnp.dot(gathered_ctx, out_weight, preferred_element_type=jnp.float32)
        + out_bias
        + tokens.astype(jnp.float32)
    )
    mean = jnp.mean(mixed, axis=1, keepdims=True)
    centered = mixed - mean
    variance = jnp.mean(centered * centered, axis=1, keepdims=True)
    normed = centered / jnp.sqrt(variance + 1e-05) * ln_gain + ln_bias
    return (normed.astype(jnp.bfloat16), kv_cache)


def solution(mesh):
    in_specs = (P(("rep", "seq"), None), P(("rep", "seq")), P(), P(), P(), P(), P())
    out_specs = (P(("rep", "seq"), None), P("rep", "seq"))
    return jax.shard_map(shards, mesh=mesh, in_specs=in_specs, out_specs=out_specs, check_vma=False)
```

```python
import math

import jax
import jax.numpy as jnp
from jax import lax
from jax.experimental import pallas as pl
from jax.experimental.pallas import tpu as pltpu
from jax.sharding import PartitionSpec as P

HEADS = 16
HEAD = 64
BQ = 512
BK = 512
INTERPRET = False


def attn_kernel(lo_ref, hi_ref, q_ref, k_ref, v_ref, sq_ref, sk_ref, o_ref):
    i = pl.program_id(0)
    q = q_ref[...]
    sq = sq_ref[...]

    def body(j, carry):
        m, l, acc = carry
        k = k_ref[j]
        v = v_ref[j]
        sk = sk_ref[j]
        s = lax.dot_general(q, k, (((1,), (1,)), ((), ())), preferred_element_type=jnp.float32)
        s = jnp.where(sq == sk, s, -jnp.inf)
        m_new = jnp.maximum(m, jnp.max(s, axis=1, keepdims=True))
        m_safe = jnp.where(m_new == -jnp.inf, 0.0, m_new)
        p = jnp.exp(s - m_safe)
        alpha = jnp.exp(m - m_safe)
        l = alpha * l + jnp.sum(p, axis=1, keepdims=True)
        acc = alpha * acc + jnp.dot(p.astype(jnp.bfloat16), v, preferred_element_type=jnp.float32)
        return m_new, l, acc

    m0 = jnp.full((BQ, 1), -jnp.inf, jnp.float32)
    l0 = jnp.zeros((BQ, 1), jnp.float32)
    acc0 = jnp.zeros((BQ, HEAD), jnp.float32)
    _, l, acc = lax.fori_loop(lo_ref[i], hi_ref[i], body, (m0, l0, acc0))
    o_ref[...] = (acc / l).astype(o_ref.dtype)


def attention(query, key_h, value_h, seg):
    rows = query.shape[0]
    nq, nk = rows // BQ, rows // BK
    first = seg[::BQ]
    last = seg[BQ - 1::BQ]
    start = jnp.sum((seg[None, :] < first[:, None]).astype(jnp.int32), axis=1)
    end = jnp.sum((seg[None, :] <= last[:, None]).astype(jnp.int32), axis=1)
    lo = start // BK
    hi = (end + BK - 1) // BK
    grid_spec = pltpu.PrefetchScalarGridSpec(
        num_scalar_prefetch=2,
        grid=(nq,),
        in_specs=[
            pl.BlockSpec((BQ, HEAD), lambda i, lo, hi: (i, 0)),
            pl.BlockSpec((nk, BK, HEAD), lambda i, lo, hi: (0, 0, 0)),
            pl.BlockSpec((nk, BK, HEAD), lambda i, lo, hi: (0, 0, 0)),
            pl.BlockSpec((BQ, 1), lambda i, lo, hi: (i, 0)),
            pl.BlockSpec((nk, 1, BK), lambda i, lo, hi: (0, 0, 0)),
        ],
        out_specs=pl.BlockSpec((BQ, HEAD), lambda i, lo, hi: (i, 0)),
    )
    return pl.pallas_call(
        attn_kernel,
        grid_spec=grid_spec,
        out_shape=jax.ShapeDtypeStruct((rows, HEAD), jnp.bfloat16),
        interpret=INTERPRET,
    )(
        lo,
        hi,
        query,
        key_h.reshape(nk, BK, HEAD),
        value_h.reshape(nk, BK, HEAD),
        seg.reshape(rows, 1),
        seg.reshape(nk, 1, BK),
    )


def shards(tokens, segments, qkv_weight, out_weight, out_bias, ln_gain, ln_bias):
    tok_rows, width = tokens.shape
    scale = 1.0 / math.sqrt(HEAD)
    all_seg = lax.all_gather(segments, "seq", axis=0, tiled=True)
    proj = jnp.dot(tokens, qkv_weight, preferred_element_type=jnp.float32).astype(jnp.bfloat16)
    grouped = proj.reshape(tok_rows, HEADS, 3 * HEAD)
    mine = lax.all_to_all(grouped, "seq", split_axis=1, concat_axis=0, tiled=True)
    count_rows = mine.shape[0]
    mine = mine.reshape(count_rows, 3 * HEAD)
    kv_cache = mine[:, HEAD:]
    query = mine[:, :HEAD] * jnp.asarray(scale, jnp.bfloat16)
    key_h = mine[:, HEAD:2 * HEAD]
    value_h = mine[:, 2 * HEAD:]
    context = attention(query, key_h, value_h, all_seg).reshape(count_rows, 1, HEAD)
    gathered_ctx = lax.all_to_all(context, "seq", split_axis=0, concat_axis=1, tiled=True)
    gathered_ctx = gathered_ctx.reshape(tok_rows, width)
    mixed = (
        jnp.dot(gathered_ctx, out_weight, preferred_element_type=jnp.float32)
        + out_bias
        + tokens.astype(jnp.float32)
    )
    mean = jnp.mean(mixed, axis=1, keepdims=True)
    centered = mixed - mean
    variance = jnp.mean(centered * centered, axis=1, keepdims=True)
    normed = centered / jnp.sqrt(variance + 1e-05) * ln_gain + ln_bias
    return (normed.astype(jnp.bfloat16), kv_cache)


def solution(mesh):
    in_specs = (P(("rep", "seq"), None), P(("rep", "seq")), P(), P(), P(), P(), P())
    out_specs = (P(("rep", "seq"), None), P("rep", "seq"))
    return jax.shard_map(shards, mesh=mesh, in_specs=in_specs, out_specs=out_specs, check_vma=False)
```

```python
import math

import jax
import jax.numpy as jnp
from jax import lax
from jax.experimental import pallas as pl
from jax.experimental.pallas import tpu as pltpu
from jax.sharding import PartitionSpec as P

HEADS = 16
HEAD = 64
SEGS = 4
BQ = 256
BK = 256
INTERPRET = False


def seg_of(x, b1, b2, b3):
    return (x >= b1).astype(jnp.int32) + (x >= b2).astype(jnp.int32) + (x >= b3).astype(jnp.int32)


def attn_kernel(lo_ref, hi_ref, bnd_ref, q_ref, kv_ref, o_ref):
    i = pl.program_id(0)
    b1, b2, b3 = bnd_ref[0], bnd_ref[1], bnd_ref[2]
    q0 = i * BQ
    scale = 1.0 / math.sqrt(HEAD)
    q = q_ref[0, :, 2 * HEAD:] * jnp.asarray(scale, jnp.bfloat16)
    rows = q0 + lax.broadcasted_iota(jnp.int32, (BQ, 1), 0)
    sq = seg_of(rows, b1, b2, b3)
    q_first = seg_of(q0, b1, b2, b3)
    q_last = seg_of(q0 + BQ - 1, b1, b2, b3)

    def tile(j, carry, masked):
        m, l, acc = carry
        kv = kv_ref[j]
        s = lax.dot_general(q, kv[:, :HEAD], (((1,), (1,)), ((), ())), preferred_element_type=jnp.float32)
        if masked:
            cols = j * BK + lax.broadcasted_iota(jnp.int32, (1, BK), 1)
            s = jnp.where(sq == seg_of(cols, b1, b2, b3), s, -jnp.inf)
        m_new = jnp.maximum(m, jnp.max(s, axis=1, keepdims=True))
        m_safe = jnp.where(m_new == -jnp.inf, 0.0, m_new)
        p = jnp.exp(s - m_safe)
        alpha = jnp.exp(m - m_safe)
        l = alpha * l + jnp.sum(p, axis=1, keepdims=True)
        acc = alpha * acc + jnp.dot(p.astype(jnp.bfloat16), kv[:, :2 * HEAD], preferred_element_type=jnp.float32)
        return m_new, l, acc

    def body(j, carry):
        k_first = seg_of(j * BK, b1, b2, b3)
        k_last = seg_of(j * BK + BK - 1, b1, b2, b3)
        inside = (q_first == q_last) & (k_first == k_last) & (q_first == k_first)
        return lax.cond(
            inside,
            lambda c: tile(j, c, False),
            lambda c: tile(j, c, True),
            carry,
        )

    m0 = jnp.full((BQ, 1), -jnp.inf, jnp.float32)
    l0 = jnp.zeros((BQ, 1), jnp.float32)
    acc0 = jnp.zeros((BQ, 2 * HEAD), jnp.float32)
    _, l, acc = lax.fori_loop(lo_ref[i], hi_ref[i], body, (m0, l0, acc0))
    out = pltpu.roll(acc / l, HEAD, 1)
    o_ref[...] = out[:, :HEAD].astype(o_ref.dtype)


def attention(mine, counts):
    nk = mine.shape[0]
    rows = nk * BK
    nq = rows // BQ
    b1, b2, b3 = counts[1], counts[2], counts[3]
    bounds = jnp.concatenate([jnp.zeros((1,), jnp.int32), counts[1:], jnp.full((1,), rows, jnp.int32)])
    starts = jnp.arange(nq, dtype=jnp.int32) * BQ
    first = seg_of(starts, b1, b2, b3)
    last = seg_of(starts + BQ - 1, b1, b2, b3)
    lo = bounds[first] // BK
    hi = (bounds[last + 1] + BK - 1) // BK
    grid_spec = pltpu.PrefetchScalarGridSpec(
        num_scalar_prefetch=3,
        grid=(nq,),
        in_specs=[
            pl.BlockSpec((1, BQ, 3 * HEAD), lambda i, lo, hi, bnd: (i, 0, 0)),
            pl.BlockSpec((nk, BK, 3 * HEAD), lambda i, lo, hi, bnd: (0, 0, 0)),
        ],
        out_specs=pl.BlockSpec((BQ, HEAD), lambda i, lo, hi, bnd: (i, 0)),
    )
    return pl.pallas_call(
        attn_kernel,
        grid_spec=grid_spec,
        out_shape=jax.ShapeDtypeStruct((rows, HEAD), jnp.bfloat16),
        interpret=INTERPRET,
    )(lo, hi, counts[1:], mine.reshape(nq, BQ, 3 * HEAD), mine)


def shards(tokens, segments, qkv_weight, out_weight, out_bias, ln_gain, ln_bias):
    tok_rows, width = tokens.shape
    groups = lax.axis_size("seq")
    levels = jnp.arange(SEGS + 1, dtype=jnp.int32)
    local = jnp.sum((segments[None, :] < levels[:, None]).astype(jnp.int32), axis=1)
    counts = lax.psum(local, "seq")
    proj = jnp.dot(tokens, qkv_weight, preferred_element_type=jnp.float32).astype(jnp.bfloat16)
    grouped = proj.reshape(tok_rows, HEADS, 3, HEAD)
    payload = jnp.concatenate([grouped[:, :, 1], grouped[:, :, 2], grouped[:, :, 0]], axis=-1)
    payload = jnp.moveaxis(payload, 1, 0)
    mine = lax.all_to_all(payload, "seq", split_axis=0, concat_axis=0, tiled=True)
    kv_cache = mine[:, :, :2 * HEAD].reshape(groups * tok_rows, 2 * HEAD)
    context = attention(mine.reshape(groups * tok_rows // BK, BK, 3 * HEAD), counts)
    ctx = lax.all_to_all(context.reshape(groups, tok_rows, HEAD), "seq", split_axis=0, concat_axis=0, tiled=True)
    mixed = (
        jnp.einsum("htc,hcd->td", ctx, out_weight.reshape(HEADS, HEAD, width), preferred_element_type=jnp.float32)
        + out_bias
        + tokens.astype(jnp.float32)
    )
    mean = jnp.mean(mixed, axis=1, keepdims=True)
    centered = mixed - mean
    variance = jnp.mean(centered * centered, axis=1, keepdims=True)
    normed = centered / jnp.sqrt(variance + 1e-05) * ln_gain + ln_bias
    return (normed.astype(jnp.bfloat16), kv_cache)


def solution(mesh):
    in_specs = (P(("rep", "seq"), None), P(("rep", "seq")), P(), P(), P(), P(), P())
    out_specs = (P(("rep", "seq"), None), P("rep", "seq"))
    return jax.shard_map(shards, mesh=mesh, in_specs=in_specs, out_specs=out_specs, check_vma=False)
```

```python
import math

import jax
import jax.numpy as jnp
from jax import lax
from jax.experimental import pallas as pl
from jax.experimental.pallas import tpu as pltpu
from jax.sharding import PartitionSpec as P

HEADS = 16
HEAD = 64
SEGS = 4
BQ = 512
BK = 512
INTERPRET = False


def seg_of(x, b1, b2, b3):
    return (x >= b1).astype(jnp.int32) + (x >= b2).astype(jnp.int32) + (x >= b3).astype(jnp.int32)


def attn_kernel(lo_ref, hi_ref, bnd_ref, q_ref, kv_ref, o_ref):
    i = pl.program_id(0)
    b1, b2, b3 = bnd_ref[0], bnd_ref[1], bnd_ref[2]
    q0 = i * BQ
    scale = 1.0 / math.sqrt(HEAD)
    q = q_ref[0, :, 2 * HEAD:] * jnp.asarray(scale, jnp.bfloat16)
    rows = q0 + lax.broadcasted_iota(jnp.int32, (BQ, 1), 0)
    sq = seg_of(rows, b1, b2, b3)

    def body(j, carry):
        m, l, acc = carry
        kv = kv_ref[j, :, :2 * HEAD]
        s = lax.dot_general(q, kv[:, :HEAD], (((1,), (1,)), ((), ())), preferred_element_type=jnp.float32)
        cols = j * BK + lax.broadcasted_iota(jnp.int32, (1, BK), 1)
        s = jnp.where(sq == seg_of(cols, b1, b2, b3), s, -jnp.inf)
        m_new = jnp.maximum(m, jnp.max(s, axis=1, keepdims=True))
        m_safe = jnp.where(m_new == -jnp.inf, 0.0, m_new)
        p = jnp.exp(s - m_safe)
        alpha = jnp.exp(m - m_safe)
        l = alpha * l + jnp.sum(p, axis=1, keepdims=True)
        acc = alpha * acc + jnp.dot(p.astype(jnp.bfloat16), kv, preferred_element_type=jnp.float32)
        return m_new, l, acc

    m0 = jnp.full((BQ, 1), -jnp.inf, jnp.float32)
    l0 = jnp.zeros((BQ, 1), jnp.float32)
    acc0 = jnp.zeros((BQ, 2 * HEAD), jnp.float32)
    _, l, acc = lax.fori_loop(lo_ref[i], hi_ref[i], body, (m0, l0, acc0))
    out = pltpu.roll(acc / l, HEAD, 1)
    o_ref[...] = out[:, :HEAD].astype(o_ref.dtype)


def attention(mine, counts):
    nk = mine.shape[0]
    rows = nk * BK
    nq = rows // BQ
    b1, b2, b3 = counts[1], counts[2], counts[3]
    bounds = jnp.concatenate([jnp.zeros((1,), jnp.int32), counts[1:], jnp.full((1,), rows, jnp.int32)])
    starts = jnp.arange(nq, dtype=jnp.int32) * BQ
    first = seg_of(starts, b1, b2, b3)
    last = seg_of(starts + BQ - 1, b1, b2, b3)
    lo = bounds[first] // BK
    hi = (bounds[last + 1] + BK - 1) // BK
    grid_spec = pltpu.PrefetchScalarGridSpec(
        num_scalar_prefetch=3,
        grid=(nq,),
        in_specs=[
            pl.BlockSpec((1, BQ, 3 * HEAD), lambda i, lo, hi, bnd: (i, 0, 0)),
            pl.BlockSpec((nk, BK, 3 * HEAD), lambda i, lo, hi, bnd: (0, 0, 0)),
        ],
        out_specs=pl.BlockSpec((BQ, HEAD), lambda i, lo, hi, bnd: (i, 0)),
    )
    return pl.pallas_call(
        attn_kernel,
        grid_spec=grid_spec,
        out_shape=jax.ShapeDtypeStruct((rows, HEAD), jnp.bfloat16),
        interpret=INTERPRET,
    )(lo, hi, counts[1:], mine.reshape(nq, BQ, 3 * HEAD), mine)


def shards(tokens, segments, qkv_weight, out_weight, out_bias, ln_gain, ln_bias):
    tok_rows, width = tokens.shape
    groups = lax.axis_size("seq")
    levels = jnp.arange(SEGS + 1, dtype=jnp.int32)
    local = jnp.sum((segments[None, :] < levels[:, None]).astype(jnp.int32), axis=1)
    counts = lax.psum(local, "seq")
    proj = jnp.dot(tokens, qkv_weight, preferred_element_type=jnp.float32).astype(jnp.bfloat16)
    grouped = proj.reshape(tok_rows, HEADS, 3, HEAD)
    payload = jnp.concatenate([grouped[:, :, 1], grouped[:, :, 2], grouped[:, :, 0]], axis=-1)
    payload = jnp.moveaxis(payload, 1, 0)
    mine = lax.all_to_all(payload, "seq", split_axis=0, concat_axis=0, tiled=True)
    kv_cache = mine[:, :, :2 * HEAD].reshape(groups * tok_rows, 2 * HEAD)
    context = attention(mine.reshape(groups * tok_rows // BK, BK, 3 * HEAD), counts)
    ctx = lax.all_to_all(context.reshape(groups, tok_rows, HEAD), "seq", split_axis=0, concat_axis=0, tiled=True)
    mixed = (
        jnp.einsum("htc,hcd->td", ctx, out_weight.reshape(HEADS, HEAD, width), preferred_element_type=jnp.float32)
        + out_bias
        + tokens.astype(jnp.float32)
    )
    mean = jnp.mean(mixed, axis=1, keepdims=True)
    centered = mixed - mean
    variance = jnp.mean(centered * centered, axis=1, keepdims=True)
    normed = centered / jnp.sqrt(variance + 1e-05) * ln_gain + ln_bias
    return (normed.astype(jnp.bfloat16), kv_cache)


def solution(mesh):
    in_specs = (P(("rep", "seq"), None), P(("rep", "seq")), P(), P(), P(), P(), P())
    out_specs = (P(("rep", "seq"), None), P("rep", "seq"))
    return jax.shard_map(shards, mesh=mesh, in_specs=in_specs, out_specs=out_specs, check_vma=False)
```

```python
import math

import jax
import jax.numpy as jnp
from jax import lax
from jax.experimental import pallas as pl
from jax.experimental.pallas import tpu as pltpu
from jax.sharding import PartitionSpec as P

HEADS = 16
HEAD = 64
SEGS = 4
BQ = 512
BK = 512
INTERPRET = False


def seg_of(x, b1, b2, b3):
    return (x >= b1).astype(jnp.int32) + (x >= b2).astype(jnp.int32) + (x >= b3).astype(jnp.int32)


def attn_kernel(lo_ref, hi_ref, bnd_ref, q_ref, kv_ref, o_ref):
    i = pl.program_id(0)
    b1, b2, b3 = bnd_ref[0], bnd_ref[1], bnd_ref[2]
    q0 = i * BQ
    scale = 1.0 / math.sqrt(HEAD)
    q = q_ref[0, :, 2 * HEAD:] * jnp.asarray(scale, jnp.bfloat16)
    rows = q0 + lax.broadcasted_iota(jnp.int32, (BQ, 1), 0)
    sq = seg_of(rows, b1, b2, b3)

    def body(j, carry):
        m, l, acc = carry
        kv = kv_ref[j, :, :2 * HEAD]
        s = lax.dot_general(q, kv[:, :HEAD], (((1,), (1,)), ((), ())), preferred_element_type=jnp.float32)
        cols = j * BK + lax.broadcasted_iota(jnp.int32, (1, BK), 1)
        s = jnp.where(sq == seg_of(cols, b1, b2, b3), s, -jnp.inf)
        m_new = jnp.maximum(m, jnp.max(s, axis=1, keepdims=True))
        m_safe = jnp.where(m_new == -jnp.inf, 0.0, m_new)
        p = jnp.exp(s - m_safe)
        alpha = jnp.exp(m - m_safe)
        l = alpha * l + jnp.sum(p, axis=1, keepdims=True)
        acc = alpha * acc + jnp.dot(p.astype(jnp.bfloat16), kv, preferred_element_type=jnp.float32)
        return m_new, l, acc

    m0 = jnp.full((BQ, 1), -jnp.inf, jnp.float32)
    l0 = jnp.zeros((BQ, 1), jnp.float32)
    acc0 = jnp.zeros((BQ, 2 * HEAD), jnp.float32)
    _, l, acc = lax.fori_loop(lo_ref[i], hi_ref[i], body, (m0, l0, acc0))
    out = pltpu.roll(acc / l, HEAD, 1)
    o_ref[...] = out[:, :HEAD].astype(o_ref.dtype)


def attention(mine, counts):
    nk = mine.shape[0]
    rows = nk * BK
    nq = rows // BQ
    b1, b2, b3 = counts[1], counts[2], counts[3]
    bounds = jnp.concatenate([jnp.zeros((1,), jnp.int32), counts[1:], jnp.full((1,), rows, jnp.int32)])
    starts = jnp.arange(nq, dtype=jnp.int32) * BQ
    first = seg_of(starts, b1, b2, b3)
    last = seg_of(starts + BQ - 1, b1, b2, b3)
    lo = bounds[first] // BK
    hi = (bounds[last + 1] + BK - 1) // BK
    grid_spec = pltpu.PrefetchScalarGridSpec(
        num_scalar_prefetch=3,
        grid=(nq,),
        in_specs=[
            pl.BlockSpec((1, BQ, 3 * HEAD), lambda i, lo, hi, bnd: (i, 0, 0)),
            pl.BlockSpec((nk, BK, 3 * HEAD), lambda i, lo, hi, bnd: (0, 0, 0)),
        ],
        out_specs=pl.BlockSpec((BQ, HEAD), lambda i, lo, hi, bnd: (i, 0)),
    )
    return pl.pallas_call(
        attn_kernel,
        grid_spec=grid_spec,
        out_shape=jax.ShapeDtypeStruct((rows, HEAD), jnp.bfloat16),
        interpret=INTERPRET,
    )(lo, hi, counts[1:], mine.reshape(nq, BQ, 3 * HEAD), mine)


def shards(tokens, segments, qkv_weight, out_weight, out_bias, ln_gain, ln_bias):
    tok_rows, width = tokens.shape
    groups = lax.axis_size("seq")
    levels = jnp.arange(SEGS + 1, dtype=jnp.int32)
    local = jnp.sum((segments[None, :] < levels[:, None]).astype(jnp.int32), axis=1)
    counts = lax.psum(local, "seq")
    counts, tokens = lax.optimization_barrier((counts, tokens))
    proj = jnp.dot(tokens, qkv_weight, preferred_element_type=jnp.float32).astype(jnp.bfloat16)
    grouped = proj.reshape(tok_rows, HEADS, 3, HEAD)
    payload = jnp.concatenate([grouped[:, :, 1], grouped[:, :, 2], grouped[:, :, 0]], axis=-1)
    payload = jnp.moveaxis(payload, 1, 0)
    mine = lax.all_to_all(payload, "seq", split_axis=0, concat_axis=0, tiled=True)
    kv_cache = mine[:, :, :2 * HEAD].reshape(groups * tok_rows, 2 * HEAD)
    context = attention(mine.reshape(groups * tok_rows // BK, BK, 3 * HEAD), counts)
    ctx = lax.all_to_all(context.reshape(groups, tok_rows, HEAD), "seq", split_axis=0, concat_axis=0, tiled=True)
    mixed = (
        jnp.einsum("htc,hcd->td", ctx, out_weight.reshape(HEADS, HEAD, width), preferred_element_type=jnp.float32)
        + out_bias
        + tokens.astype(jnp.float32)
    )
    mean = jnp.mean(mixed, axis=1, keepdims=True)
    centered = mixed - mean
    variance = jnp.mean(centered * centered, axis=1, keepdims=True)
    normed = centered / jnp.sqrt(variance + 1e-05) * ln_gain + ln_bias
    return (normed.astype(jnp.bfloat16), kv_cache)


def solution(mesh):
    in_specs = (P(("rep", "seq"), None), P(("rep", "seq")), P(), P(), P(), P(), P())
    out_specs = (P(("rep", "seq"), None), P("rep", "seq"))
    return jax.shard_map(shards, mesh=mesh, in_specs=in_specs, out_specs=out_specs, check_vma=False)
```

```python
import math

import jax
import jax.numpy as jnp
from jax import lax
from jax.experimental import pallas as pl
from jax.experimental.pallas import tpu as pltpu
from jax.sharding import PartitionSpec as P

HEADS = 16
HEAD = 64
SEGS = 4
BQ = 512
BK = 512
INTERPRET = False


def seg_of(x, b1, b2, b3):
    return (x >= b1).astype(jnp.int32) + (x >= b2).astype(jnp.int32) + (x >= b3).astype(jnp.int32)


def attn_kernel(lo_ref, hi_ref, bnd_ref, q_ref, kv_ref, o_ref):
    i = pl.program_id(0)
    b1, b2, b3 = bnd_ref[0], bnd_ref[1], bnd_ref[2]
    q0 = i * BQ
    scale = 1.0 / math.sqrt(HEAD)
    q = q_ref[0, :, 2 * HEAD:] * jnp.asarray(scale, jnp.bfloat16)
    rows = q0 + lax.broadcasted_iota(jnp.int32, (BQ, 1), 0)
    sq = seg_of(rows, b1, b2, b3)

    def body(j, carry):
        m, l, acc = carry
        kv = kv_ref[j, :, :2 * HEAD]
        s = lax.dot_general(q, kv[:, :HEAD], (((1,), (1,)), ((), ())), preferred_element_type=jnp.float32)
        cols = j * BK + lax.broadcasted_iota(jnp.int32, (1, BK), 1)
        s = jnp.where(sq == seg_of(cols, b1, b2, b3), s, -jnp.inf)
        m_new = jnp.maximum(m, jnp.max(s, axis=1, keepdims=True))
        m_safe = jnp.where(m_new == -jnp.inf, 0.0, m_new)
        p = jnp.exp(s - m_safe)
        alpha = jnp.exp(m - m_safe)
        l = alpha * l + jnp.sum(p, axis=1, keepdims=True)
        acc = alpha * acc + jnp.dot(p.astype(jnp.bfloat16), kv, preferred_element_type=jnp.float32)
        return m_new, l, acc

    m0 = jnp.full((BQ, 1), -jnp.inf, jnp.float32)
    l0 = jnp.zeros((BQ, 1), jnp.float32)
    acc0 = jnp.zeros((BQ, 2 * HEAD), jnp.float32)
    _, l, acc = lax.fori_loop(lo_ref[i], hi_ref[i], body, (m0, l0, acc0))
    out = pltpu.roll(acc / l, HEAD, 1)
    o_ref[...] = out[:, :HEAD].astype(o_ref.dtype)


def attention(mine, counts):
    nk = mine.shape[0]
    rows = nk * BK
    nq = rows // BQ
    b1, b2, b3 = counts[1], counts[2], counts[3]
    bounds = jnp.concatenate([jnp.zeros((1,), jnp.int32), counts[1:], jnp.full((1,), rows, jnp.int32)])
    starts = jnp.arange(nq, dtype=jnp.int32) * BQ
    first = seg_of(starts, b1, b2, b3)
    last = seg_of(starts + BQ - 1, b1, b2, b3)
    lo = bounds[first] // BK
    hi = (bounds[last + 1] + BK - 1) // BK
    grid_spec = pltpu.PrefetchScalarGridSpec(
        num_scalar_prefetch=3,
        grid=(nq,),
        in_specs=[
            pl.BlockSpec((1, BQ, 3 * HEAD), lambda i, lo, hi, bnd: (i, 0, 0)),
            pl.BlockSpec((nk, BK, 3 * HEAD), lambda i, lo, hi, bnd: (0, 0, 0)),
        ],
        out_specs=pl.BlockSpec((BQ, HEAD), lambda i, lo, hi, bnd: (i, 0)),
    )
    return pl.pallas_call(
        attn_kernel,
        grid_spec=grid_spec,
        out_shape=jax.ShapeDtypeStruct((rows, HEAD), jnp.bfloat16),
        interpret=INTERPRET,
    )(lo, hi, counts[1:], mine.reshape(nq, BQ, 3 * HEAD), mine)


def shards(tokens, segments, qkv_weight, out_weight, out_bias, ln_gain, ln_bias):
    tok_rows, width = tokens.shape
    groups = lax.axis_size("seq")
    levels = jnp.arange(SEGS + 1, dtype=jnp.int32)
    local = jnp.sum((segments[None, :] < levels[:, None]).astype(jnp.int32), axis=1)
    counts = local
    for shift in range(1, groups):
        pairs = [(d, (d + shift) % groups) for d in range(groups)]
        counts = counts + lax.ppermute(local, "seq", pairs)
    counts, tokens = lax.optimization_barrier((counts, tokens))
    proj = jnp.dot(tokens, qkv_weight, preferred_element_type=jnp.float32).astype(jnp.bfloat16)
    grouped = proj.reshape(tok_rows, HEADS, 3, HEAD)
    payload = jnp.concatenate([grouped[:, :, 1], grouped[:, :, 2], grouped[:, :, 0]], axis=-1)
    payload = jnp.moveaxis(payload, 1, 0)
    mine = lax.all_to_all(payload, "seq", split_axis=0, concat_axis=0, tiled=True)
    kv_cache = mine[:, :, :2 * HEAD].reshape(groups * tok_rows, 2 * HEAD)
    context = attention(mine.reshape(groups * tok_rows // BK, BK, 3 * HEAD), counts)
    ctx = lax.all_to_all(context.reshape(groups, tok_rows, HEAD), "seq", split_axis=0, concat_axis=0, tiled=True)
    mixed = (
        jnp.einsum("htc,hcd->td", ctx, out_weight.reshape(HEADS, HEAD, width), preferred_element_type=jnp.float32)
        + out_bias
        + tokens.astype(jnp.float32)
    )
    mean = jnp.mean(mixed, axis=1, keepdims=True)
    centered = mixed - mean
    variance = jnp.mean(centered * centered, axis=1, keepdims=True)
    normed = centered / jnp.sqrt(variance + 1e-05) * ln_gain + ln_bias
    return (normed.astype(jnp.bfloat16), kv_cache)


def solution(mesh):
    in_specs = (P(("rep", "seq"), None), P(("rep", "seq")), P(), P(), P(), P(), P())
    out_specs = (P(("rep", "seq"), None), P("rep", "seq"))
    return jax.shard_map(shards, mesh=mesh, in_specs=in_specs, out_specs=out_specs, check_vma=False)
```

```python
import math

import jax
import jax.numpy as jnp
from jax import lax
from jax.experimental import pallas as pl
from jax.experimental.pallas import tpu as pltpu
from jax.sharding import PartitionSpec as P

HEADS = 16
HEAD = 64
SEGS = 4
BQ = 512
BK = 512
INTERPRET = False


def seg_of(x, b1, b2, b3):
    return (x >= b1).astype(jnp.int32) + (x >= b2).astype(jnp.int32) + (x >= b3).astype(jnp.int32)


def attn_kernel(cnt_ref, q_ref, kv_ref, o_ref):
    i = pl.program_id(0)
    b1, b2, b3 = cnt_ref[1], cnt_ref[2], cnt_ref[3]
    q0 = i * BQ
    first = seg_of(q0, b1, b2, b3)
    last = seg_of(q0 + BQ - 1, b1, b2, b3)
    lo = cnt_ref[first] // BK
    hi = (cnt_ref[last + 1] + BK - 1) // BK
    scale = 1.0 / math.sqrt(HEAD)
    q = q_ref[0, :, 2 * HEAD:3 * HEAD] * jnp.asarray(scale, jnp.bfloat16)
    rows = q0 + lax.broadcasted_iota(jnp.int32, (BQ, 1), 0)
    sq = seg_of(rows, b1, b2, b3)

    def body(j, carry):
        m, l, acc = carry
        kv = kv_ref[j, :, :2 * HEAD]
        s = lax.dot_general(q, kv[:, :HEAD], (((1,), (1,)), ((), ())), preferred_element_type=jnp.float32)
        cols = j * BK + lax.broadcasted_iota(jnp.int32, (1, BK), 1)
        s = jnp.where(sq == seg_of(cols, b1, b2, b3), s, -jnp.inf)
        m_new = jnp.maximum(m, jnp.max(s, axis=1, keepdims=True))
        m_safe = jnp.where(m_new == -jnp.inf, 0.0, m_new)
        p = jnp.exp(s - m_safe)
        alpha = jnp.exp(m - m_safe)
        l = alpha * l + jnp.sum(p, axis=1, keepdims=True)
        acc = alpha * acc + jnp.dot(p.astype(jnp.bfloat16), kv, preferred_element_type=jnp.float32)
        return m_new, l, acc

    m0 = jnp.full((BQ, 1), -jnp.inf, jnp.float32)
    l0 = jnp.zeros((BQ, 1), jnp.float32)
    acc0 = jnp.zeros((BQ, 2 * HEAD), jnp.float32)
    _, l, acc = lax.fori_loop(lo, hi, body, (m0, l0, acc0))
    out = pltpu.roll(acc / l, HEAD, 1)
    o_ref[...] = out[:, :HEAD].astype(o_ref.dtype)


def attention(mine, counts):
    nk, _, feat = mine.shape
    rows = nk * BK
    nq = rows // BQ
    grid_spec = pltpu.PrefetchScalarGridSpec(
        num_scalar_prefetch=1,
        grid=(nq,),
        in_specs=[
            pl.BlockSpec((1, BQ, feat), lambda i, cnt: (i, 0, 0)),
            pl.BlockSpec((nk, BK, feat), lambda i, cnt: (0, 0, 0)),
        ],
        out_specs=pl.BlockSpec((BQ, HEAD), lambda i, cnt: (i, 0)),
    )
    return pl.pallas_call(
        attn_kernel,
        grid_spec=grid_spec,
        out_shape=jax.ShapeDtypeStruct((rows, HEAD), jnp.bfloat16),
        interpret=INTERPRET,
    )(counts, mine.reshape(nq, BQ, feat), mine)


def shards(tokens, segments, qkv_weight, out_weight, out_bias, ln_gain, ln_bias):
    tok_rows, width = tokens.shape
    groups = lax.axis_size("seq")
    proj = jnp.dot(tokens, qkv_weight, preferred_element_type=jnp.float32).astype(jnp.bfloat16)
    grouped = proj.reshape(tok_rows, HEADS, 3, HEAD)
    seg_col = jnp.broadcast_to(segments.astype(jnp.bfloat16)[:, None, None], (tok_rows, HEADS, 1))
    payload = jnp.concatenate([grouped[:, :, 1], grouped[:, :, 2], grouped[:, :, 0], seg_col], axis=-1)
    payload = jnp.moveaxis(payload, 1, 0)
    mine = lax.all_to_all(payload, "seq", split_axis=0, concat_axis=0, tiled=True)
    kv_cache = mine[:, :, :2 * HEAD].reshape(groups * tok_rows, 2 * HEAD)
    all_seg = mine[:, :, 3 * HEAD].astype(jnp.int32).reshape(groups * tok_rows)
    levels = jnp.arange(SEGS + 1, dtype=jnp.int32)
    counts = jnp.sum((all_seg[None, :] < levels[:, None]).astype(jnp.int32), axis=1)
    context = attention(mine.reshape(groups * tok_rows // BK, BK, 3 * HEAD + 1), counts)
    ctx = lax.all_to_all(context.reshape(groups, tok_rows, HEAD), "seq", split_axis=0, concat_axis=0, tiled=True)
    mixed = (
        jnp.einsum("htc,hcd->td", ctx, out_weight.reshape(HEADS, HEAD, width), preferred_element_type=jnp.float32)
        + out_bias
        + tokens.astype(jnp.float32)
    )
    mean = jnp.mean(mixed, axis=1, keepdims=True)
    centered = mixed - mean
    variance = jnp.mean(centered * centered, axis=1, keepdims=True)
    normed = centered / jnp.sqrt(variance + 1e-05) * ln_gain + ln_bias
    return (normed.astype(jnp.bfloat16), kv_cache)


def solution(mesh):
    in_specs = (P(("rep", "seq"), None), P(("rep", "seq")), P(), P(), P(), P(), P())
    out_specs = (P(("rep", "seq"), None), P("rep", "seq"))
    return jax.shard_map(shards, mesh=mesh, in_specs=in_specs, out_specs=out_specs, check_vma=False)
```

```python
import math

import jax
import jax.numpy as jnp
from jax import lax
from jax.experimental import pallas as pl
from jax.experimental.pallas import tpu as pltpu
from jax.sharding import PartitionSpec as P

HEADS = 16
HEAD = 64
SEGS = 4
BQ = 512
BK = 512
INTERPRET = False


def seg_of(x, b1, b2, b3):
    return (x >= b1).astype(jnp.int32) + (x >= b2).astype(jnp.int32) + (x >= b3).astype(jnp.int32)


def attn_kernel(cnt_ref, q_ref, kv_ref, o_ref):
    i = pl.program_id(0)
    b1, b2, b3 = cnt_ref[1], cnt_ref[2], cnt_ref[3]
    q0 = i * BQ
    first = seg_of(q0, b1, b2, b3)
    last = seg_of(q0 + BQ - 1, b1, b2, b3)
    start = cnt_ref[first]
    end = cnt_ref[last + 1]
    lo = start // BK
    hi = (end + BK - 1) // BK
    inside = first == last
    mid_lo = jnp.where(inside, (start + BK - 1) // BK, hi)
    mid_hi = jnp.where(inside, jnp.maximum(end // BK, mid_lo), hi)
    scale = 1.0 / math.sqrt(HEAD)
    q = q_ref[0, :, 2 * HEAD:3 * HEAD] * jnp.asarray(scale, jnp.bfloat16)
    rows = q0 + lax.broadcasted_iota(jnp.int32, (BQ, 1), 0)
    sq = seg_of(rows, b1, b2, b3)

    def tile(j, carry, masked):
        m, l, acc = carry
        kv = kv_ref[j, :, :2 * HEAD]
        s = lax.dot_general(q, kv[:, :HEAD], (((1,), (1,)), ((), ())), preferred_element_type=jnp.float32)
        if masked:
            cols = j * BK + lax.broadcasted_iota(jnp.int32, (1, BK), 1)
            s = jnp.where(sq == seg_of(cols, b1, b2, b3), s, -jnp.inf)
        m_new = jnp.maximum(m, jnp.max(s, axis=1, keepdims=True))
        m_safe = jnp.where(m_new == -jnp.inf, 0.0, m_new)
        p = jnp.exp(s - m_safe)
        alpha = jnp.exp(m - m_safe)
        l = alpha * l + jnp.sum(p, axis=1, keepdims=True)
        acc = alpha * acc + jnp.dot(p.astype(jnp.bfloat16), kv, preferred_element_type=jnp.float32)
        return m_new, l, acc

    def masked_tile(j, carry):
        return tile(j, carry, True)

    def plain_tile(j, carry):
        return tile(j, carry, False)

    m0 = jnp.full((BQ, 1), -jnp.inf, jnp.float32)
    l0 = jnp.zeros((BQ, 1), jnp.float32)
    acc0 = jnp.zeros((BQ, 2 * HEAD), jnp.float32)
    carry = lax.fori_loop(lo, mid_lo, masked_tile, (m0, l0, acc0))
    carry = lax.fori_loop(mid_lo, mid_hi, plain_tile, carry)
    _, l, acc = lax.fori_loop(mid_hi, hi, masked_tile, carry)
    out = pltpu.roll(acc / l, HEAD, 1)
    o_ref[...] = out[:, :HEAD].astype(o_ref.dtype)


def attention(mine, counts):
    nk, _, feat = mine.shape
    rows = nk * BK
    nq = rows // BQ
    grid_spec = pltpu.PrefetchScalarGridSpec(
        num_scalar_prefetch=1,
        grid=(nq,),
        in_specs=[
            pl.BlockSpec((1, BQ, feat), lambda i, cnt: (i, 0, 0)),
            pl.BlockSpec((nk, BK, feat), lambda i, cnt: (0, 0, 0)),
        ],
        out_specs=pl.BlockSpec((BQ, HEAD), lambda i, cnt: (i, 0)),
    )
    return pl.pallas_call(
        attn_kernel,
        grid_spec=grid_spec,
        out_shape=jax.ShapeDtypeStruct((rows, HEAD), jnp.bfloat16),
        interpret=INTERPRET,
    )(counts, mine.reshape(nq, BQ, feat), mine)


def shards(tokens, segments, qkv_weight, out_weight, out_bias, ln_gain, ln_bias):
    tok_rows, width = tokens.shape
    groups = lax.axis_size("seq")
    proj = jnp.dot(tokens, qkv_weight, preferred_element_type=jnp.float32).astype(jnp.bfloat16)
    grouped = proj.reshape(tok_rows, HEADS, 3, HEAD)
    seg_col = jnp.broadcast_to(segments.astype(jnp.bfloat16)[:, None, None], (tok_rows, HEADS, 1))
    payload = jnp.concatenate([grouped[:, :, 1], grouped[:, :, 2], grouped[:, :, 0], seg_col], axis=-1)
    payload = jnp.moveaxis(payload, 1, 0)
    mine = lax.all_to_all(payload, "seq", split_axis=0, concat_axis=0, tiled=True)
    kv_cache = mine[:, :, :2 * HEAD].reshape(groups * tok_rows, 2 * HEAD)
    all_seg = mine[:, :, 3 * HEAD].astype(jnp.int32).reshape(groups * tok_rows)
    levels = jnp.arange(SEGS + 1, dtype=jnp.int32)
    counts = jnp.sum((all_seg[None, :] < levels[:, None]).astype(jnp.int32), axis=1)
    context = attention(mine.reshape(groups * tok_rows // BK, BK, 3 * HEAD + 1), counts)
    ctx = lax.all_to_all(context.reshape(groups, tok_rows, HEAD), "seq", split_axis=0, concat_axis=0, tiled=True)
    mixed = (
        jnp.einsum("htc,hcd->td", ctx, out_weight.reshape(HEADS, HEAD, width), preferred_element_type=jnp.float32)
        + out_bias
        + tokens.astype(jnp.float32)
    )
    mean = jnp.mean(mixed, axis=1, keepdims=True)
    centered = mixed - mean
    variance = jnp.mean(centered * centered, axis=1, keepdims=True)
    normed = centered / jnp.sqrt(variance + 1e-05) * ln_gain + ln_bias
    return (normed.astype(jnp.bfloat16), kv_cache)


def solution(mesh):
    in_specs = (P(("rep", "seq"), None), P(("rep", "seq")), P(), P(), P(), P(), P())
    out_specs = (P(("rep", "seq"), None), P("rep", "seq"))
    return jax.shard_map(shards, mesh=mesh, in_specs=in_specs, out_specs=out_specs, check_vma=False)
```

```python
import math

import jax
import jax.numpy as jnp
from jax import lax
from jax.experimental import pallas as pl
from jax.experimental.pallas import tpu as pltpu
from jax.sharding import PartitionSpec as P

HEADS = 16
HEAD = 64
SEGS = 4
BQ = 512
BK = 256
INTERPRET = False


def seg_of(x, b1, b2, b3):
    return (x >= b1).astype(jnp.int32) + (x >= b2).astype(jnp.int32) + (x >= b3).astype(jnp.int32)


def attn_kernel(cnt_ref, q_ref, kv_ref, o_ref):
    i = pl.program_id(0)
    b1, b2, b3 = cnt_ref[1], cnt_ref[2], cnt_ref[3]
    q0 = i * BQ
    first = seg_of(q0, b1, b2, b3)
    last = seg_of(q0 + BQ - 1, b1, b2, b3)
    start = cnt_ref[first]
    end = cnt_ref[last + 1]
    lo = start // BK
    hi = (end + BK - 1) // BK
    inside = first == last
    mid_lo = jnp.where(inside, (start + BK - 1) // BK, hi)
    mid_hi = jnp.where(inside, jnp.maximum(end // BK, mid_lo), hi)
    scale = 1.0 / math.sqrt(HEAD)
    q = q_ref[0, :, 2 * HEAD:3 * HEAD] * jnp.asarray(scale, jnp.bfloat16)
    rows = q0 + lax.broadcasted_iota(jnp.int32, (BQ, 1), 0)
    sq = seg_of(rows, b1, b2, b3)

    def tile(j, carry, masked):
        m, l, acc = carry
        kv = kv_ref[j, :, :2 * HEAD]
        s = lax.dot_general(q, kv[:, :HEAD], (((1,), (1,)), ((), ())), preferred_element_type=jnp.float32)
        if masked:
            cols = j * BK + lax.broadcasted_iota(jnp.int32, (1, BK), 1)
            s = jnp.where(sq == seg_of(cols, b1, b2, b3), s, -jnp.inf)
        m_new = jnp.maximum(m, jnp.max(s, axis=1, keepdims=True))
        m_safe = jnp.where(m_new == -jnp.inf, 0.0, m_new)
        p = jnp.exp(s - m_safe)
        alpha = jnp.exp(m - m_safe)
        l = alpha * l + jnp.sum(p, axis=1, keepdims=True)
        acc = alpha * acc + jnp.dot(p.astype(jnp.bfloat16), kv, preferred_element_type=jnp.float32)
        return m_new, l, acc

    def masked_tile(j, carry):
        return tile(j, carry, True)

    def plain_tile(j, carry):
        return tile(j, carry, False)

    m0 = jnp.full((BQ, 1), -jnp.inf, jnp.float32)
    l0 = jnp.zeros((BQ, 1), jnp.float32)
    acc0 = jnp.zeros((BQ, 2 * HEAD), jnp.float32)
    carry = lax.fori_loop(lo, mid_lo, masked_tile, (m0, l0, acc0))
    carry = lax.fori_loop(mid_lo, mid_hi, plain_tile, carry)
    _, l, acc = lax.fori_loop(mid_hi, hi, masked_tile, carry)
    out = pltpu.roll(acc / l, HEAD, 1)
    o_ref[...] = out[:, :HEAD].astype(o_ref.dtype)


def attention(mine, counts):
    nk, _, feat = mine.shape
    rows = nk * BK
    nq = rows // BQ
    grid_spec = pltpu.PrefetchScalarGridSpec(
        num_scalar_prefetch=1,
        grid=(nq,),
        in_specs=[
            pl.BlockSpec((1, BQ, feat), lambda i, cnt: (i, 0, 0)),
            pl.BlockSpec((nk, BK, feat), lambda i, cnt: (0, 0, 0)),
        ],
        out_specs=pl.BlockSpec((BQ, HEAD), lambda i, cnt: (i, 0)),
    )
    return pl.pallas_call(
        attn_kernel,
        grid_spec=grid_spec,
        out_shape=jax.ShapeDtypeStruct((rows, HEAD), jnp.bfloat16),
        interpret=INTERPRET,
    )(counts, mine.reshape(nq, BQ, feat), mine)


def shards(tokens, segments, qkv_weight, out_weight, out_bias, ln_gain, ln_bias):
    tok_rows, width = tokens.shape
    groups = lax.axis_size("seq")
    proj = jnp.dot(tokens, qkv_weight, preferred_element_type=jnp.float32).astype(jnp.bfloat16)
    grouped = proj.reshape(tok_rows, HEADS, 3, HEAD)
    seg_col = jnp.broadcast_to(segments.astype(jnp.bfloat16)[:, None, None], (tok_rows, HEADS, 1))
    payload = jnp.concatenate([grouped[:, :, 1], grouped[:, :, 2], grouped[:, :, 0], seg_col], axis=-1)
    payload = jnp.moveaxis(payload, 1, 0)
    mine = lax.all_to_all(payload, "seq", split_axis=0, concat_axis=0, tiled=True)
    kv_cache = mine[:, :, :2 * HEAD].reshape(groups * tok_rows, 2 * HEAD)
    all_seg = mine[:, :, 3 * HEAD].astype(jnp.int32).reshape(groups * tok_rows)
    levels = jnp.arange(SEGS + 1, dtype=jnp.int32)
    counts = jnp.sum((all_seg[None, :] < levels[:, None]).astype(jnp.int32), axis=1)
    context = attention(mine.reshape(groups * tok_rows // BK, BK, 3 * HEAD + 1), counts)
    ctx = lax.all_to_all(context.reshape(groups, tok_rows, HEAD), "seq", split_axis=0, concat_axis=0, tiled=True)
    mixed = (
        jnp.einsum("htc,hcd->td", ctx, out_weight.reshape(HEADS, HEAD, width), preferred_element_type=jnp.float32)
        + out_bias
        + tokens.astype(jnp.float32)
    )
    mean = jnp.mean(mixed, axis=1, keepdims=True)
    centered = mixed - mean
    variance = jnp.mean(centered * centered, axis=1, keepdims=True)
    normed = centered / jnp.sqrt(variance + 1e-05) * ln_gain + ln_bias
    return (normed.astype(jnp.bfloat16), kv_cache)


def solution(mesh):
    in_specs = (P(("rep", "seq"), None), P(("rep", "seq")), P(), P(), P(), P(), P())
    out_specs = (P(("rep", "seq"), None), P("rep", "seq"))
    return jax.shard_map(shards, mesh=mesh, in_specs=in_specs, out_specs=out_specs, check_vma=False)
```

```python
import math

import jax
import jax.numpy as jnp
from jax import lax
from jax.experimental import pallas as pl
from jax.experimental.pallas import tpu as pltpu
from jax.sharding import PartitionSpec as P

HEADS = 16
HEAD = 64
SEGS = 4
BQ = 512
BK = 1024
INTERPRET = False


def seg_of(x, b1, b2, b3):
    return (x >= b1).astype(jnp.int32) + (x >= b2).astype(jnp.int32) + (x >= b3).astype(jnp.int32)


def attn_kernel(cnt_ref, q_ref, kv_ref, o_ref):
    i = pl.program_id(0)
    b1, b2, b3 = cnt_ref[1], cnt_ref[2], cnt_ref[3]
    q0 = i * BQ
    first = seg_of(q0, b1, b2, b3)
    last = seg_of(q0 + BQ - 1, b1, b2, b3)
    start = cnt_ref[first]
    end = cnt_ref[last + 1]
    lo = start // BK
    hi = (end + BK - 1) // BK
    inside = first == last
    mid_lo = jnp.where(inside, (start + BK - 1) // BK, hi)
    mid_hi = jnp.where(inside, jnp.maximum(end // BK, mid_lo), hi)
    scale = 1.0 / math.sqrt(HEAD)
    q = q_ref[0, :, 2 * HEAD:3 * HEAD] * jnp.asarray(scale, jnp.bfloat16)
    rows = q0 + lax.broadcasted_iota(jnp.int32, (BQ, 1), 0)
    sq = seg_of(rows, b1, b2, b3)

    def tile(j, carry, masked):
        m, l, acc = carry
        kv = kv_ref[j, :, :2 * HEAD]
        s = lax.dot_general(q, kv[:, :HEAD], (((1,), (1,)), ((), ())), preferred_element_type=jnp.float32)
        if masked:
            cols = j * BK + lax.broadcasted_iota(jnp.int32, (1, BK), 1)
            s = jnp.where(sq == seg_of(cols, b1, b2, b3), s, -jnp.inf)
        m_new = jnp.maximum(m, jnp.max(s, axis=1, keepdims=True))
        m_safe = jnp.where(m_new == -jnp.inf, 0.0, m_new)
        p = jnp.exp(s - m_safe)
        alpha = jnp.exp(m - m_safe)
        l = alpha * l + jnp.sum(p, axis=1, keepdims=True)
        acc = alpha * acc + jnp.dot(p.astype(jnp.bfloat16), kv, preferred_element_type=jnp.float32)
        return m_new, l, acc

    def masked_tile(j, carry):
        return tile(j, carry, True)

    def plain_tile(j, carry):
        return tile(j, carry, False)

    m0 = jnp.full((BQ, 1), -jnp.inf, jnp.float32)
    l0 = jnp.zeros((BQ, 1), jnp.float32)
    acc0 = jnp.zeros((BQ, 2 * HEAD), jnp.float32)
    carry = lax.fori_loop(lo, mid_lo, masked_tile, (m0, l0, acc0))
    carry = lax.fori_loop(mid_lo, mid_hi, plain_tile, carry)
    _, l, acc = lax.fori_loop(mid_hi, hi, masked_tile, carry)
    out = pltpu.roll(acc / l, HEAD, 1)
    o_ref[...] = out[:, :HEAD].astype(o_ref.dtype)


def attention(mine, counts):
    nk, _, feat = mine.shape
    rows = nk * BK
    nq = rows // BQ
    grid_spec = pltpu.PrefetchScalarGridSpec(
        num_scalar_prefetch=1,
        grid=(nq,),
        in_specs=[
            pl.BlockSpec((1, BQ, feat), lambda i, cnt: (i, 0, 0)),
            pl.BlockSpec((nk, BK, feat), lambda i, cnt: (0, 0, 0)),
        ],
        out_specs=pl.BlockSpec((BQ, HEAD), lambda i, cnt: (i, 0)),
    )
    return pl.pallas_call(
        attn_kernel,
        grid_spec=grid_spec,
        out_shape=jax.ShapeDtypeStruct((rows, HEAD), jnp.bfloat16),
        interpret=INTERPRET,
    )(counts, mine.reshape(nq, BQ, feat), mine)


def shards(tokens, segments, qkv_weight, out_weight, out_bias, ln_gain, ln_bias):
    tok_rows, width = tokens.shape
    groups = lax.axis_size("seq")
    proj = jnp.dot(tokens, qkv_weight, preferred_element_type=jnp.float32).astype(jnp.bfloat16)
    grouped = proj.reshape(tok_rows, HEADS, 3, HEAD)
    seg_col = jnp.broadcast_to(segments.astype(jnp.bfloat16)[:, None, None], (tok_rows, HEADS, 1))
    payload = jnp.concatenate([grouped[:, :, 1], grouped[:, :, 2], grouped[:, :, 0], seg_col], axis=-1)
    payload = jnp.moveaxis(payload, 1, 0)
    mine = lax.all_to_all(payload, "seq", split_axis=0, concat_axis=0, tiled=True)
    kv_cache = mine[:, :, :2 * HEAD].reshape(groups * tok_rows, 2 * HEAD)
    all_seg = mine[:, :, 3 * HEAD].astype(jnp.int32).reshape(groups * tok_rows)
    levels = jnp.arange(SEGS + 1, dtype=jnp.int32)
    counts = jnp.sum((all_seg[None, :] < levels[:, None]).astype(jnp.int32), axis=1)
    context = attention(mine.reshape(groups * tok_rows // BK, BK, 3 * HEAD + 1), counts)
    ctx = lax.all_to_all(context.reshape(groups, tok_rows, HEAD), "seq", split_axis=0, concat_axis=0, tiled=True)
    mixed = (
        jnp.einsum("htc,hcd->td", ctx, out_weight.reshape(HEADS, HEAD, width), preferred_element_type=jnp.float32)
        + out_bias
        + tokens.astype(jnp.float32)
    )
    mean = jnp.mean(mixed, axis=1, keepdims=True)
    centered = mixed - mean
    variance = jnp.mean(centered * centered, axis=1, keepdims=True)
    normed = centered / jnp.sqrt(variance + 1e-05) * ln_gain + ln_bias
    return (normed.astype(jnp.bfloat16), kv_cache)


def solution(mesh):
    in_specs = (P(("rep", "seq"), None), P(("rep", "seq")), P(), P(), P(), P(), P())
    out_specs = (P(("rep", "seq"), None), P("rep", "seq"))
    return jax.shard_map(shards, mesh=mesh, in_specs=in_specs, out_specs=out_specs, check_vma=False)
```

```python
import math

import jax
import jax.numpy as jnp
from jax import lax
from jax.experimental import pallas as pl
from jax.experimental.pallas import tpu as pltpu
from jax.sharding import PartitionSpec as P

HEADS = 16
HEAD = 64
SEGS = 4
BQ = 512
BK = 1024
INTERPRET = False


def seg_of(x, b1, b2, b3):
    return (x >= b1).astype(jnp.int32) + (x >= b2).astype(jnp.int32) + (x >= b3).astype(jnp.int32)


def attn_kernel(cnt_ref, q_ref, kv_ref, o_ref):
    i = pl.program_id(0)
    b1, b2, b3 = cnt_ref[1], cnt_ref[2], cnt_ref[3]
    q0 = i * BQ
    first = seg_of(q0, b1, b2, b3)
    last = seg_of(q0 + BQ - 1, b1, b2, b3)
    start = cnt_ref[first]
    end = cnt_ref[last + 1]
    lo = start // BK
    hi = (end + BK - 1) // BK
    inside = first == last
    mid_lo = jnp.where(inside, (start + BK - 1) // BK, hi)
    mid_hi = jnp.where(inside, jnp.maximum(end // BK, mid_lo), hi)
    scale = 1.0 / math.sqrt(HEAD)
    q = q_ref[0, :, 2 * HEAD:3 * HEAD] * jnp.asarray(scale, jnp.bfloat16)
    rows = q0 + lax.broadcasted_iota(jnp.int32, (BQ, 1), 0)
    sq = seg_of(rows, b1, b2, b3)

    def tile(j, carry, masked):
        m, l, acc = carry
        kv = kv_ref[j, :, :2 * HEAD]
        s = lax.dot_general(q, kv[:, :HEAD], (((1,), (1,)), ((), ())), preferred_element_type=jnp.float32)
        if masked:
            cols = j * BK + lax.broadcasted_iota(jnp.int32, (1, BK), 1)
            s = jnp.where(sq == seg_of(cols, b1, b2, b3), s, -jnp.inf)
        m_new = jnp.maximum(m, jnp.max(s, axis=1, keepdims=True))
        m_safe = jnp.where(m_new == -jnp.inf, 0.0, m_new)
        p = jnp.exp(s - m_safe)
        alpha = jnp.exp(m - m_safe)
        l = alpha * l + jnp.sum(p, axis=1, keepdims=True)
        acc = alpha * acc + jnp.dot(p.astype(jnp.bfloat16), kv, preferred_element_type=jnp.float32)
        return m_new, l, acc

    def masked_tile(j, carry):
        return tile(j, carry, True)

    def plain_tile(j, carry):
        return tile(j, carry, False)

    m0 = jnp.full((BQ, 1), -jnp.inf, jnp.float32)
    l0 = jnp.zeros((BQ, 1), jnp.float32)
    acc0 = jnp.zeros((BQ, 2 * HEAD), jnp.float32)
    carry = lax.fori_loop(lo, mid_lo, masked_tile, (m0, l0, acc0))
    carry = lax.fori_loop(mid_lo, mid_hi, plain_tile, carry)
    _, l, acc = lax.fori_loop(mid_hi, hi, masked_tile, carry)
    out = pltpu.roll(acc / l, HEAD, 1)
    o_ref[...] = out[:, :HEAD].astype(o_ref.dtype)


def attention(mine, counts):
    nk, _, feat = mine.shape
    rows = nk * BK
    nq = rows // BQ
    grid_spec = pltpu.PrefetchScalarGridSpec(
        num_scalar_prefetch=1,
        grid=(nq,),
        in_specs=[
            pl.BlockSpec((1, BQ, feat), lambda i, cnt: (i, 0, 0)),
            pl.BlockSpec((nk, BK, feat), lambda i, cnt: (0, 0, 0)),
        ],
        out_specs=pl.BlockSpec((BQ, HEAD), lambda i, cnt: (i, 0)),
    )
    return pl.pallas_call(
        attn_kernel,
        grid_spec=grid_spec,
        out_shape=jax.ShapeDtypeStruct((rows, HEAD), jnp.bfloat16),
        interpret=INTERPRET,
    )(counts, mine.reshape(nq, BQ, feat), mine)


def shards(tokens, segments, qkv_weight, out_weight, out_bias, ln_gain, ln_bias):
    tok_rows, width = tokens.shape
    groups = lax.axis_size("seq")
    proj_t = jnp.einsum("td,dc->ct", tokens, qkv_weight, preferred_element_type=jnp.float32).astype(jnp.bfloat16)
    grouped = proj_t.reshape(HEADS, 3, HEAD, tok_rows)
    seg_row = jnp.broadcast_to(segments.astype(jnp.bfloat16)[None, None, :], (HEADS, 1, tok_rows))
    payload = jnp.concatenate([grouped[:, 1], grouped[:, 2], grouped[:, 0], seg_row], axis=1)
    mine_t = lax.all_to_all(payload, "seq", split_axis=0, concat_axis=0, tiled=True)
    mine = jnp.swapaxes(mine_t, 1, 2)
    kv_cache = mine[:, :, :2 * HEAD].reshape(groups * tok_rows, 2 * HEAD)
    all_seg = mine[:, :, 3 * HEAD].astype(jnp.int32).reshape(groups * tok_rows)
    levels = jnp.arange(SEGS + 1, dtype=jnp.int32)
    counts = jnp.sum((all_seg[None, :] < levels[:, None]).astype(jnp.int32), axis=1)
    context = attention(mine.reshape(groups * tok_rows // BK, BK, 3 * HEAD + 1), counts)
    ctx = lax.all_to_all(context.reshape(groups, tok_rows, HEAD), "seq", split_axis=0, concat_axis=0, tiled=True)
    mixed = (
        jnp.einsum("htc,hcd->td", ctx, out_weight.reshape(HEADS, HEAD, width), preferred_element_type=jnp.float32)
        + out_bias
        + tokens.astype(jnp.float32)
    )
    mean = jnp.mean(mixed, axis=1, keepdims=True)
    centered = mixed - mean
    variance = jnp.mean(centered * centered, axis=1, keepdims=True)
    normed = centered / jnp.sqrt(variance + 1e-05) * ln_gain + ln_bias
    return (normed.astype(jnp.bfloat16), kv_cache)


def solution(mesh):
    in_specs = (P(("rep", "seq"), None), P(("rep", "seq")), P(), P(), P(), P(), P())
    out_specs = (P(("rep", "seq"), None), P("rep", "seq"))
    return jax.shard_map(shards, mesh=mesh, in_specs=in_specs, out_specs=out_specs, check_vma=False)
```

```python
import math

import jax
import jax.numpy as jnp
from jax import lax
from jax.experimental import pallas as pl
from jax.experimental.pallas import tpu as pltpu
from jax.sharding import PartitionSpec as P

HEADS = 16
HEAD = 64
SEGS = 4
BQ = 512
BK = 1024
INTERPRET = False


def seg_of(x, b1, b2, b3):
    return (x >= b1).astype(jnp.int32) + (x >= b2).astype(jnp.int32) + (x >= b3).astype(jnp.int32)


def attn_kernel(cnt_ref, q_ref, kv_ref, o_ref):
    i = pl.program_id(0)
    b1, b2, b3 = cnt_ref[1], cnt_ref[2], cnt_ref[3]
    q0 = i * BQ
    first = seg_of(q0, b1, b2, b3)
    last = seg_of(q0 + BQ - 1, b1, b2, b3)
    start = cnt_ref[first]
    end = cnt_ref[last + 1]
    lo = start // BK
    hi = (end + BK - 1) // BK
    inside = first == last
    mid_lo = jnp.where(inside, (start + BK - 1) // BK, hi)
    mid_hi = jnp.where(inside, jnp.maximum(end // BK, mid_lo), hi)
    scale = 1.0 / math.sqrt(HEAD)
    q = q_ref[0, :, 2 * HEAD:3 * HEAD] * jnp.asarray(scale, jnp.bfloat16)
    rows = q0 + lax.broadcasted_iota(jnp.int32, (BQ, 1), 0)
    sq = seg_of(rows, b1, b2, b3)

    def tile(j, carry, masked):
        m, l, acc = carry
        kv = kv_ref[j, :, :2 * HEAD]
        s = lax.dot_general(q, kv[:, :HEAD], (((1,), (1,)), ((), ())), preferred_element_type=jnp.float32)
        if masked:
            cols = j * BK + lax.broadcasted_iota(jnp.int32, (1, BK), 1)
            s = jnp.where(sq == seg_of(cols, b1, b2, b3), s, -jnp.inf)
        m_new = jnp.maximum(m, jnp.max(s, axis=1, keepdims=True))
        m_safe = jnp.where(m_new == -jnp.inf, 0.0, m_new)
        p = jnp.exp(s - m_safe)
        alpha = jnp.exp(m - m_safe)
        l = alpha * l + jnp.sum(p, axis=1, keepdims=True)
        acc = alpha * acc + jnp.dot(p.astype(jnp.bfloat16), kv, preferred_element_type=jnp.float32)
        return m_new, l, acc

    def masked_tile(j, carry):
        return tile(j, carry, True)

    def plain_tile(j, carry):
        return tile(j, carry, False)

    m0 = jnp.full((BQ, 1), -jnp.inf, jnp.float32)
    l0 = jnp.zeros((BQ, 1), jnp.float32)
    acc0 = jnp.zeros((BQ, 2 * HEAD), jnp.float32)
    carry = lax.fori_loop(lo, mid_lo, masked_tile, (m0, l0, acc0))
    carry = lax.fori_loop(mid_lo, mid_hi, plain_tile, carry)
    _, l, acc = lax.fori_loop(mid_hi, hi, masked_tile, carry)
    out = jnp.transpose(acc / l)[HEAD:, :].astype(o_ref.dtype)
    per = o_ref.shape[2]
    for b in range(BQ // per):
        o_ref[b] = out[:, b * per:(b + 1) * per]


def attention(mine, counts, tok_rows):
    nk, _, feat = mine.shape
    rows = nk * BK
    nq = rows // BQ
    grid_spec = pltpu.PrefetchScalarGridSpec(
        num_scalar_prefetch=1,
        grid=(nq,),
        in_specs=[
            pl.BlockSpec((1, BQ, feat), lambda i, cnt: (i, 0, 0)),
            pl.BlockSpec((nk, BK, feat), lambda i, cnt: (0, 0, 0)),
        ],
        out_specs=pl.BlockSpec((BQ // tok_rows, HEAD, tok_rows), lambda i, cnt: (i, 0, 0)),
    )
    return pl.pallas_call(
        attn_kernel,
        grid_spec=grid_spec,
        out_shape=jax.ShapeDtypeStruct((rows // tok_rows, HEAD, tok_rows), jnp.bfloat16),
        interpret=INTERPRET,
    )(counts, mine.reshape(nq, BQ, feat), mine)


def shards(tokens, segments, qkv_weight, out_weight, out_bias, ln_gain, ln_bias):
    tok_rows, width = tokens.shape
    groups = lax.axis_size("seq")
    proj_t = jnp.einsum("td,dc->ct", tokens, qkv_weight, preferred_element_type=jnp.float32).astype(jnp.bfloat16)
    grouped = proj_t.reshape(HEADS, 3, HEAD, tok_rows)
    seg_row = jnp.broadcast_to(segments.astype(jnp.bfloat16)[None, None, :], (HEADS, 1, tok_rows))
    payload = jnp.concatenate([grouped[:, 1], grouped[:, 2], grouped[:, 0], seg_row], axis=1)
    mine_t = lax.all_to_all(payload, "seq", split_axis=0, concat_axis=0, tiled=True)
    mine = jnp.swapaxes(mine_t, 1, 2)
    kv_cache = mine[:, :, :2 * HEAD].reshape(groups * tok_rows, 2 * HEAD)
    all_seg = mine_t[:, 3 * HEAD, :].astype(jnp.int32).reshape(groups * tok_rows)
    levels = jnp.arange(SEGS + 1, dtype=jnp.int32)
    counts = jnp.sum((all_seg[None, :] < levels[:, None]).astype(jnp.int32), axis=1)
    context = attention(mine.reshape(groups * tok_rows // BK, BK, 3 * HEAD + 1), counts, tok_rows)
    ctx = lax.all_to_all(context, "seq", split_axis=0, concat_axis=0, tiled=True)
    mixed = (
        jnp.einsum("hct,hcd->td", ctx, out_weight.reshape(HEADS, HEAD, width), preferred_element_type=jnp.float32)
        + out_bias
        + tokens.astype(jnp.float32)
    )
    mean = jnp.mean(mixed, axis=1, keepdims=True)
    centered = mixed - mean
    variance = jnp.mean(centered * centered, axis=1, keepdims=True)
    normed = centered / jnp.sqrt(variance + 1e-05) * ln_gain + ln_bias
    return (normed.astype(jnp.bfloat16), kv_cache)


def solution(mesh):
    in_specs = (P(("rep", "seq"), None), P(("rep", "seq")), P(), P(), P(), P(), P())
    out_specs = (P(("rep", "seq"), None), P("rep", "seq"))
    return jax.shard_map(shards, mesh=mesh, in_specs=in_specs, out_specs=out_specs, check_vma=False)
```

```python
import math

import jax
import jax.numpy as jnp
from jax import lax
from jax.experimental import pallas as pl
from jax.experimental.pallas import tpu as pltpu
from jax.sharding import PartitionSpec as P

HEADS = 16
HEAD = 64
SEGS = 4
BQ = 512
BK = 1024
INTERPRET = False


def seg_of(x, b1, b2, b3):
    return (x >= b1).astype(jnp.int32) + (x >= b2).astype(jnp.int32) + (x >= b3).astype(jnp.int32)


def attn_kernel(cnt_ref, q_ref, kv_ref, o_ref):
    i = pl.program_id(0)
    b1, b2, b3 = cnt_ref[1], cnt_ref[2], cnt_ref[3]
    q0 = i * BQ
    first = seg_of(q0, b1, b2, b3)
    last = seg_of(q0 + BQ - 1, b1, b2, b3)
    start = cnt_ref[first]
    end = cnt_ref[last + 1]
    lo = start // BK
    hi = (end + BK - 1) // BK
    inside = first == last
    mid_lo = jnp.where(inside, (start + BK - 1) // BK, hi)
    mid_hi = jnp.where(inside, jnp.maximum(end // BK, mid_lo), hi)
    scale = 1.0 / math.sqrt(HEAD)
    q = q_ref[0, :, 3 * HEAD:4 * HEAD] * jnp.asarray(scale, jnp.bfloat16)
    rows = q0 + lax.broadcasted_iota(jnp.int32, (BQ, 1), 0)
    sq = seg_of(rows, b1, b2, b3)

    def tile(j, carry, masked):
        m, acc = carry
        kv = kv_ref[j, :, :2 * HEAD]
        k = kv_ref[j, :, 2 * HEAD:3 * HEAD]
        s = lax.dot_general(q, k, (((1,), (1,)), ((), ())), preferred_element_type=jnp.float32)
        if masked:
            cols = j * BK + lax.broadcasted_iota(jnp.int32, (1, BK), 1)
            s = jnp.where(sq == seg_of(cols, b1, b2, b3), s, -jnp.inf)
        m_new = jnp.maximum(m, jnp.max(s, axis=1, keepdims=True))
        m_safe = jnp.where(m_new == -jnp.inf, 0.0, m_new)
        p = jnp.exp(s - m_safe)
        alpha = jnp.exp(m - m_safe)
        acc = alpha * acc + jnp.dot(p.astype(jnp.bfloat16), kv, preferred_element_type=jnp.float32)
        return m_new, acc

    def masked_tile(j, carry):
        return tile(j, carry, True)

    def plain_tile(j, carry):
        return tile(j, carry, False)

    m0 = jnp.full((BQ, 1), -jnp.inf, jnp.float32)
    acc0 = jnp.zeros((BQ, 2 * HEAD), jnp.float32)
    carry = lax.fori_loop(lo, mid_lo, masked_tile, (m0, acc0))
    carry = lax.fori_loop(mid_lo, mid_hi, plain_tile, carry)
    _, acc = lax.fori_loop(mid_hi, hi, masked_tile, carry)
    out = jnp.transpose(acc / acc[:, :1])[HEAD:, :].astype(o_ref.dtype)
    per = o_ref.shape[2]
    for b in range(BQ // per):
        o_ref[b] = out[:, b * per:(b + 1) * per]


def attention(mine, counts, tok_rows):
    nk, _, feat = mine.shape
    rows = nk * BK
    nq = rows // BQ
    grid_spec = pltpu.PrefetchScalarGridSpec(
        num_scalar_prefetch=1,
        grid=(nq,),
        in_specs=[
            pl.BlockSpec((1, BQ, feat), lambda i, cnt: (i, 0, 0)),
            pl.BlockSpec((nk, BK, feat), lambda i, cnt: (0, 0, 0)),
        ],
        out_specs=pl.BlockSpec((BQ // tok_rows, HEAD, tok_rows), lambda i, cnt: (i, 0, 0)),
    )
    return pl.pallas_call(
        attn_kernel,
        grid_spec=grid_spec,
        out_shape=jax.ShapeDtypeStruct((rows // tok_rows, HEAD, tok_rows), jnp.bfloat16),
        interpret=INTERPRET,
    )(counts, mine.reshape(nq, BQ, feat), mine)


def shards(tokens, segments, qkv_weight, out_weight, out_bias, ln_gain, ln_bias):
    tok_rows, width = tokens.shape
    groups = lax.axis_size("seq")
    proj_t = jnp.einsum("td,dc->ct", tokens, qkv_weight, preferred_element_type=jnp.float32).astype(jnp.bfloat16)
    grouped = proj_t.reshape(HEADS, 3, HEAD, tok_rows)
    seg_row = jnp.broadcast_to(segments.astype(jnp.bfloat16)[None, None, :], (HEADS, 1, tok_rows))
    payload = jnp.concatenate([grouped[:, 1], grouped[:, 2], grouped[:, 0], seg_row], axis=1)
    mine_t = lax.all_to_all(payload, "seq", split_axis=0, concat_axis=0, tiled=True)
    mine = jnp.swapaxes(mine_t, 1, 2)
    kv_cache = mine[:, :, :2 * HEAD].reshape(groups * tok_rows, 2 * HEAD)
    all_seg = mine_t[:, 3 * HEAD, :].astype(jnp.int32).reshape(groups * tok_rows)
    levels = jnp.arange(SEGS + 1, dtype=jnp.int32)
    counts = jnp.sum((all_seg[None, :] < levels[:, None]).astype(jnp.int32), axis=1)
    ones = jnp.ones((groups, HEAD, tok_rows), jnp.bfloat16)
    kernel_t = jnp.concatenate([ones, mine_t[:, HEAD:2 * HEAD], mine_t[:, :HEAD], mine_t[:, 2 * HEAD:3 * HEAD]], axis=1)
    kernel_in = jnp.swapaxes(kernel_t, 1, 2).reshape(groups * tok_rows // BK, BK, 4 * HEAD)
    context = attention(kernel_in, counts, tok_rows)
    ctx = lax.all_to_all(context, "seq", split_axis=0, concat_axis=0, tiled=True)
    mixed = (
        jnp.einsum("hct,hcd->td", ctx, out_weight.reshape(HEADS, HEAD, width), preferred_element_type=jnp.float32)
        + out_bias
        + tokens.astype(jnp.float32)
    )
    mean = jnp.mean(mixed, axis=1, keepdims=True)
    centered = mixed - mean
    variance = jnp.mean(centered * centered, axis=1, keepdims=True)
    normed = centered / jnp.sqrt(variance + 1e-05) * ln_gain + ln_bias
    return (normed.astype(jnp.bfloat16), kv_cache)


def solution(mesh):
    in_specs = (P(("rep", "seq"), None), P(("rep", "seq")), P(), P(), P(), P(), P())
    out_specs = (P(("rep", "seq"), None), P("rep", "seq"))
    return jax.shard_map(shards, mesh=mesh, in_specs=in_specs, out_specs=out_specs, check_vma=False)
```

```python
import math

import jax
import jax.numpy as jnp
from jax import lax
from jax.experimental import pallas as pl
from jax.experimental.pallas import tpu as pltpu
from jax.sharding import PartitionSpec as P

HEADS = 16
HEAD = 64
SEGS = 4
BQ = 512
BK = 1024
INTERPRET = False


def seg_of(x, b1, b2, b3):
    return (x >= b1).astype(jnp.int32) + (x >= b2).astype(jnp.int32) + (x >= b3).astype(jnp.int32)


def attn_kernel(cnt_ref, q_ref, kv_ref, o_ref):
    i = pl.program_id(0)
    b1, b2, b3 = cnt_ref[1], cnt_ref[2], cnt_ref[3]
    q0 = i * BQ
    first = seg_of(q0, b1, b2, b3)
    last = seg_of(q0 + BQ - 1, b1, b2, b3)
    start = cnt_ref[first]
    end = cnt_ref[last + 1]
    lo = start // BK
    hi = (end + BK - 1) // BK
    inside = first == last
    mid_lo = jnp.where(inside, (start + BK - 1) // BK, hi)
    mid_hi = jnp.where(inside, jnp.maximum(end // BK, mid_lo), hi)
    scale = 1.0 / math.sqrt(HEAD)
    q = q_ref[0, :, 2 * HEAD:3 * HEAD] * jnp.asarray(scale, jnp.bfloat16)
    rows = q0 + lax.broadcasted_iota(jnp.int32, (BQ, 1), 0)
    sq = seg_of(rows, b1, b2, b3)

    key_lanes = lax.broadcasted_iota(jnp.int32, (BK, 2 * HEAD), 1) < HEAD

    def tile(j, carry, masked):
        m, acc = carry
        kv = kv_ref[j, :, :2 * HEAD]
        s = lax.dot_general(q, kv[:, :HEAD], (((1,), (1,)), ((), ())), preferred_element_type=jnp.float32)
        if masked:
            cols = j * BK + lax.broadcasted_iota(jnp.int32, (1, BK), 1)
            s = jnp.where(sq == seg_of(cols, b1, b2, b3), s, -jnp.inf)
        m_new = jnp.maximum(m, jnp.max(s, axis=1, keepdims=True))
        m_safe = jnp.where(m_new == -jnp.inf, 0.0, m_new)
        p = jnp.exp(s - m_safe)
        alpha = jnp.exp(m - m_safe)
        rhs = jnp.where(key_lanes, jnp.ones_like(kv), kv)
        acc = alpha * acc + jnp.dot(p.astype(jnp.bfloat16), rhs, preferred_element_type=jnp.float32)
        return m_new, acc

    def masked_tile(j, carry):
        return tile(j, carry, True)

    def plain_tile(j, carry):
        return tile(j, carry, False)

    m0 = jnp.full((BQ, 1), -jnp.inf, jnp.float32)
    acc0 = jnp.zeros((BQ, 2 * HEAD), jnp.float32)
    carry = lax.fori_loop(lo, mid_lo, masked_tile, (m0, acc0))
    carry = lax.fori_loop(mid_lo, mid_hi, plain_tile, carry)
    _, acc = lax.fori_loop(mid_hi, hi, masked_tile, carry)
    out = jnp.transpose(acc / acc[:, :1])[HEAD:, :].astype(o_ref.dtype)
    per = o_ref.shape[2]
    for b in range(BQ // per):
        o_ref[b] = out[:, b * per:(b + 1) * per]


def attention(mine, counts, tok_rows):
    nk, _, feat = mine.shape
    rows = nk * BK
    nq = rows // BQ
    grid_spec = pltpu.PrefetchScalarGridSpec(
        num_scalar_prefetch=1,
        grid=(nq,),
        in_specs=[
            pl.BlockSpec((1, BQ, feat), lambda i, cnt: (i, 0, 0)),
            pl.BlockSpec((nk, BK, feat), lambda i, cnt: (0, 0, 0)),
        ],
        out_specs=pl.BlockSpec((BQ // tok_rows, HEAD, tok_rows), lambda i, cnt: (i, 0, 0)),
    )
    return pl.pallas_call(
        attn_kernel,
        grid_spec=grid_spec,
        out_shape=jax.ShapeDtypeStruct((rows // tok_rows, HEAD, tok_rows), jnp.bfloat16),
        interpret=INTERPRET,
    )(counts, mine.reshape(nq, BQ, feat), mine)


def shards(tokens, segments, qkv_weight, out_weight, out_bias, ln_gain, ln_bias):
    tok_rows, width = tokens.shape
    groups = lax.axis_size("seq")
    proj_t = jnp.einsum("td,dc->ct", tokens, qkv_weight, preferred_element_type=jnp.float32).astype(jnp.bfloat16)
    grouped = proj_t.reshape(HEADS, 3, HEAD, tok_rows)
    seg_row = jnp.broadcast_to(segments.astype(jnp.bfloat16)[None, None, :], (HEADS, 1, tok_rows))
    payload = jnp.concatenate([grouped[:, 1], grouped[:, 2], grouped[:, 0], seg_row], axis=1)
    mine_t = lax.all_to_all(payload, "seq", split_axis=0, concat_axis=0, tiled=True)
    mine = jnp.swapaxes(mine_t, 1, 2)
    kv_cache = mine[:, :, :2 * HEAD].reshape(groups * tok_rows, 2 * HEAD)
    all_seg = mine_t[:, 3 * HEAD, :].astype(jnp.int32).reshape(groups * tok_rows)
    levels = jnp.arange(SEGS + 1, dtype=jnp.int32)
    counts = jnp.sum((all_seg[None, :] < levels[:, None]).astype(jnp.int32), axis=1)
    context = attention(mine.reshape(groups * tok_rows // BK, BK, 3 * HEAD + 1), counts, tok_rows)
    ctx = lax.all_to_all(context, "seq", split_axis=0, concat_axis=0, tiled=True)
    mixed = (
        jnp.einsum("hct,hcd->td", ctx, out_weight.reshape(HEADS, HEAD, width), preferred_element_type=jnp.float32)
        + out_bias
        + tokens.astype(jnp.float32)
    )
    mean = jnp.mean(mixed, axis=1, keepdims=True)
    centered = mixed - mean
    variance = jnp.mean(centered * centered, axis=1, keepdims=True)
    normed = centered / jnp.sqrt(variance + 1e-05) * ln_gain + ln_bias
    return (normed.astype(jnp.bfloat16), kv_cache)


def solution(mesh):
    in_specs = (P(("rep", "seq"), None), P(("rep", "seq")), P(), P(), P(), P(), P())
    out_specs = (P(("rep", "seq"), None), P("rep", "seq"))
    return jax.shard_map(shards, mesh=mesh, in_specs=in_specs, out_specs=out_specs, check_vma=False)
```

```python
import math

import jax
import jax.numpy as jnp
from jax import lax
from jax.experimental import pallas as pl
from jax.experimental.pallas import tpu as pltpu
from jax.sharding import PartitionSpec as P

HEADS = 16
HEAD = 64
SEGS = 4
BQ = 512
BK = 1024
INTERPRET = False


def seg_of(x, b1, b2, b3):
    return (x >= b1).astype(jnp.int32) + (x >= b2).astype(jnp.int32) + (x >= b3).astype(jnp.int32)


def attn_kernel(cnt_ref, q_ref, kv_ref, o_ref):
    i = pl.program_id(0)
    b1, b2, b3 = cnt_ref[1], cnt_ref[2], cnt_ref[3]
    q0 = i * BQ
    first = seg_of(q0, b1, b2, b3)
    last = seg_of(q0 + BQ - 1, b1, b2, b3)
    start = cnt_ref[first]
    end = cnt_ref[last + 1]
    lo = start // BK
    hi = (end + BK - 1) // BK
    inside = first == last
    mid_lo = jnp.where(inside, (start + BK - 1) // BK, hi)
    mid_hi = jnp.where(inside, jnp.maximum(end // BK, mid_lo), hi)
    scale = 1.0 / math.sqrt(HEAD)
    q = q_ref[0, :, 2 * HEAD:3 * HEAD] * jnp.asarray(scale, jnp.bfloat16)
    rows = q0 + lax.broadcasted_iota(jnp.int32, (BQ, 1), 0)
    sq = seg_of(rows, b1, b2, b3)

    key_lanes = lax.broadcasted_iota(jnp.int32, (BK, 2 * HEAD), 1) < HEAD

    def tile(j, carry, masked):
        m, acc = carry
        kv = kv_ref[j, :, :2 * HEAD]
        s = lax.dot_general(q, kv[:, :HEAD], (((1,), (1,)), ((), ())), preferred_element_type=jnp.float32)
        if masked:
            cols = j * BK + lax.broadcasted_iota(jnp.int32, (1, BK), 1)
            s = jnp.where(sq == seg_of(cols, b1, b2, b3), s, -jnp.inf)
        m_new = jnp.maximum(m, jnp.max(s, axis=1, keepdims=True))
        p = jnp.exp(s - m_new)
        alpha = jnp.exp(m - m_new)
        rhs = jnp.where(key_lanes, jnp.ones_like(kv), kv)
        acc = alpha * acc + jnp.dot(p.astype(jnp.bfloat16), rhs, preferred_element_type=jnp.float32)
        return m_new, acc

    def masked_tile(j, carry):
        return tile(j, carry, True)

    def plain_tile(j, carry):
        return tile(j, carry, False)

    m0 = jnp.full((BQ, 1), -1e30, jnp.float32)
    acc0 = jnp.zeros((BQ, 2 * HEAD), jnp.float32)
    carry = lax.fori_loop(lo, mid_lo, masked_tile, (m0, acc0))
    carry = lax.fori_loop(mid_lo, mid_hi, plain_tile, carry)
    _, acc = lax.fori_loop(mid_hi, hi, masked_tile, carry)
    out = jnp.transpose(acc / acc[:, :1])[HEAD:, :].astype(o_ref.dtype)
    per = o_ref.shape[2]
    for b in range(BQ // per):
        o_ref[b] = out[:, b * per:(b + 1) * per]


def attention(mine, counts, tok_rows):
    nk, _, feat = mine.shape
    rows = nk * BK
    nq = rows // BQ
    grid_spec = pltpu.PrefetchScalarGridSpec(
        num_scalar_prefetch=1,
        grid=(nq,),
        in_specs=[
            pl.BlockSpec((1, BQ, feat), lambda i, cnt: (i, 0, 0)),
            pl.BlockSpec((nk, BK, feat), lambda i, cnt: (0, 0, 0)),
        ],
        out_specs=pl.BlockSpec((BQ // tok_rows, HEAD, tok_rows), lambda i, cnt: (i, 0, 0)),
    )
    return pl.pallas_call(
        attn_kernel,
        grid_spec=grid_spec,
        out_shape=jax.ShapeDtypeStruct((rows // tok_rows, HEAD, tok_rows), jnp.bfloat16),
        interpret=INTERPRET,
    )(counts, mine.reshape(nq, BQ, feat), mine)


def shards(tokens, segments, qkv_weight, out_weight, out_bias, ln_gain, ln_bias):
    tok_rows, width = tokens.shape
    groups = lax.axis_size("seq")
    proj_t = jnp.einsum("td,dc->ct", tokens, qkv_weight, preferred_element_type=jnp.float32).astype(jnp.bfloat16)
    grouped = proj_t.reshape(HEADS, 3, HEAD, tok_rows)
    seg_row = jnp.broadcast_to(segments.astype(jnp.bfloat16)[None, None, :], (HEADS, 1, tok_rows))
    payload = jnp.concatenate([grouped[:, 1], grouped[:, 2], grouped[:, 0], seg_row], axis=1)
    mine_t = lax.all_to_all(payload, "seq", split_axis=0, concat_axis=0, tiled=True)
    mine = jnp.swapaxes(mine_t, 1, 2)
    kv_cache = mine[:, :, :2 * HEAD].reshape(groups * tok_rows, 2 * HEAD)
    all_seg = mine_t[:, 3 * HEAD, :].astype(jnp.int32).reshape(groups * tok_rows)
    levels = jnp.arange(SEGS + 1, dtype=jnp.int32)
    counts = jnp.sum((all_seg[None, :] < levels[:, None]).astype(jnp.int32), axis=1)
    context = attention(mine.reshape(groups * tok_rows // BK, BK, 3 * HEAD + 1), counts, tok_rows)
    ctx = lax.all_to_all(context, "seq", split_axis=0, concat_axis=0, tiled=True)
    mixed = (
        jnp.einsum("hct,hcd->td", ctx, out_weight.reshape(HEADS, HEAD, width), preferred_element_type=jnp.float32)
        + out_bias
        + tokens.astype(jnp.float32)
    )
    mean = jnp.mean(mixed, axis=1, keepdims=True)
    centered = mixed - mean
    variance = jnp.mean(centered * centered, axis=1, keepdims=True)
    normed = centered / jnp.sqrt(variance + 1e-05) * ln_gain + ln_bias
    return (normed.astype(jnp.bfloat16), kv_cache)


def solution(mesh):
    in_specs = (P(("rep", "seq"), None), P(("rep", "seq")), P(), P(), P(), P(), P())
    out_specs = (P(("rep", "seq"), None), P("rep", "seq"))
    return jax.shard_map(shards, mesh=mesh, in_specs=in_specs, out_specs=out_specs, check_vma=False)
```

```python
import math

import jax
import jax.numpy as jnp
from jax import lax
from jax.experimental import pallas as pl
from jax.experimental.pallas import tpu as pltpu
from jax.sharding import PartitionSpec as P

HEADS = 16
HEAD = 64
SEGS = 4
BQ = 512
BK = 1024
INTERPRET = False


def seg_of(x, b1, b2, b3):
    return (x >= b1).astype(jnp.int32) + (x >= b2).astype(jnp.int32) + (x >= b3).astype(jnp.int32)


def attn_kernel(cnt_ref, q_ref, kv_ref, o_ref, pv_ref):
    i = pl.program_id(0)
    b1, b2, b3 = cnt_ref[1], cnt_ref[2], cnt_ref[3]
    q0 = i * BQ
    first = seg_of(q0, b1, b2, b3)
    last = seg_of(q0 + BQ - 1, b1, b2, b3)
    start = cnt_ref[first]
    end = cnt_ref[last + 1]
    lo = start // BK
    hi = (end + BK - 1) // BK
    inside = first == last
    mid_lo = jnp.where(inside, (start + BK - 1) // BK, hi)
    mid_hi = jnp.where(inside, jnp.maximum(end // BK, mid_lo), hi)
    scale = 1.0 / math.sqrt(HEAD)
    q = q_ref[0, :, 2 * HEAD:3 * HEAD] * jnp.asarray(scale, jnp.bfloat16)
    rows = q0 + lax.broadcasted_iota(jnp.int32, (BQ, 1), 0)
    sq = seg_of(rows, b1, b2, b3)

    @pl.when(i == 0)
    def _():
        key_lanes = lax.broadcasted_iota(jnp.int32, (BK, 2 * HEAD), 1) < HEAD
        for b in range(pv_ref.shape[0]):
            block = kv_ref[b, :, :2 * HEAD]
            pv_ref[b] = jnp.where(key_lanes, jnp.ones_like(block), block)

    def tile(j, carry, masked):
        m, acc = carry
        k = kv_ref[j, :, :HEAD]
        s = lax.dot_general(q, k, (((1,), (1,)), ((), ())), preferred_element_type=jnp.float32)
        if masked:
            cols = j * BK + lax.broadcasted_iota(jnp.int32, (1, BK), 1)
            s = jnp.where(sq == seg_of(cols, b1, b2, b3), s, -jnp.inf)
        m_new = jnp.maximum(m, jnp.max(s, axis=1, keepdims=True))
        p = jnp.exp(s - m_new)
        alpha = jnp.exp(m - m_new)
        acc = alpha * acc + jnp.dot(p.astype(jnp.bfloat16), pv_ref[j], preferred_element_type=jnp.float32)
        return m_new, acc

    def masked_tile(j, carry):
        return tile(j, carry, True)

    def plain_tile(j, carry):
        return tile(j, carry, False)

    m0 = jnp.full((BQ, 1), -1e30, jnp.float32)
    acc0 = jnp.zeros((BQ, 2 * HEAD), jnp.float32)
    carry = lax.fori_loop(lo, mid_lo, masked_tile, (m0, acc0))
    carry = lax.fori_loop(mid_lo, mid_hi, plain_tile, carry)
    _, acc = lax.fori_loop(mid_hi, hi, masked_tile, carry)
    out = jnp.transpose(acc / acc[:, :1])[HEAD:, :].astype(o_ref.dtype)
    per = o_ref.shape[2]
    for b in range(BQ // per):
        o_ref[b] = out[:, b * per:(b + 1) * per]


def attention(mine, counts, tok_rows):
    nk, _, feat = mine.shape
    rows = nk * BK
    nq = rows // BQ
    grid_spec = pltpu.PrefetchScalarGridSpec(
        num_scalar_prefetch=1,
        grid=(nq,),
        in_specs=[
            pl.BlockSpec((1, BQ, feat), lambda i, cnt: (i, 0, 0)),
            pl.BlockSpec((nk, BK, feat), lambda i, cnt: (0, 0, 0)),
        ],
        out_specs=pl.BlockSpec((BQ // tok_rows, HEAD, tok_rows), lambda i, cnt: (i, 0, 0)),
        scratch_shapes=[pltpu.VMEM((nk, BK, 2 * HEAD), jnp.bfloat16)],
    )
    return pl.pallas_call(
        attn_kernel,
        grid_spec=grid_spec,
        out_shape=jax.ShapeDtypeStruct((rows // tok_rows, HEAD, tok_rows), jnp.bfloat16),
        interpret=INTERPRET,
    )(counts, mine.reshape(nq, BQ, feat), mine)


def shards(tokens, segments, qkv_weight, out_weight, out_bias, ln_gain, ln_bias):
    tok_rows, width = tokens.shape
    groups = lax.axis_size("seq")
    proj_t = jnp.einsum("td,dc->ct", tokens, qkv_weight, preferred_element_type=jnp.float32).astype(jnp.bfloat16)
    grouped = proj_t.reshape(HEADS, 3, HEAD, tok_rows)
    seg_row = jnp.broadcast_to(segments.astype(jnp.bfloat16)[None, None, :], (HEADS, 1, tok_rows))
    payload = jnp.concatenate([grouped[:, 1], grouped[:, 2], grouped[:, 0], seg_row], axis=1)
    mine_t = lax.all_to_all(payload, "seq", split_axis=0, concat_axis=0, tiled=True)
    mine = jnp.swapaxes(mine_t, 1, 2)
    kv_cache = mine[:, :, :2 * HEAD].reshape(groups * tok_rows, 2 * HEAD)
    all_seg = mine_t[:, 3 * HEAD, :].astype(jnp.int32).reshape(groups * tok_rows)
    levels = jnp.arange(SEGS + 1, dtype=jnp.int32)
    counts = jnp.sum((all_seg[None, :] < levels[:, None]).astype(jnp.int32), axis=1)
    context = attention(mine.reshape(groups * tok_rows // BK, BK, 3 * HEAD + 1), counts, tok_rows)
    ctx = lax.all_to_all(context, "seq", split_axis=0, concat_axis=0, tiled=True)
    mixed = (
        jnp.einsum("hct,hcd->td", ctx, out_weight.reshape(HEADS, HEAD, width), preferred_element_type=jnp.float32)
        + out_bias
        + tokens.astype(jnp.float32)
    )
    mean = jnp.mean(mixed, axis=1, keepdims=True)
    centered = mixed - mean
    variance = jnp.mean(centered * centered, axis=1, keepdims=True)
    normed = centered / jnp.sqrt(variance + 1e-05) * ln_gain + ln_bias
    return (normed.astype(jnp.bfloat16), kv_cache)


def solution(mesh):
    in_specs = (P(("rep", "seq"), None), P(("rep", "seq")), P(), P(), P(), P(), P())
    out_specs = (P(("rep", "seq"), None), P("rep", "seq"))
    return jax.shard_map(shards, mesh=mesh, in_specs=in_specs, out_specs=out_specs, check_vma=False)
```

```python
import math

import jax
import jax.numpy as jnp
from jax import lax
from jax.experimental import pallas as pl
from jax.experimental.pallas import tpu as pltpu
from jax.sharding import PartitionSpec as P

HEADS = 16
HEAD = 64
SEGS = 4
BQ = 1024
BK = 1024
INTERPRET = False


def seg_of(x, b1, b2, b3):
    return (x >= b1).astype(jnp.int32) + (x >= b2).astype(jnp.int32) + (x >= b3).astype(jnp.int32)


def attn_kernel(cnt_ref, q_ref, kv_ref, o_ref):
    i = pl.program_id(0)
    b1, b2, b3 = cnt_ref[1], cnt_ref[2], cnt_ref[3]
    q0 = i * BQ
    first = seg_of(q0, b1, b2, b3)
    last = seg_of(q0 + BQ - 1, b1, b2, b3)
    start = cnt_ref[first]
    end = cnt_ref[last + 1]
    lo = start // BK
    hi = (end + BK - 1) // BK
    inside = first == last
    mid_lo = jnp.where(inside, (start + BK - 1) // BK, hi)
    mid_hi = jnp.where(inside, jnp.maximum(end // BK, mid_lo), hi)
    scale = 1.0 / math.sqrt(HEAD)
    q = q_ref[0, :, 2 * HEAD:3 * HEAD] * jnp.asarray(scale, jnp.bfloat16)
    rows = q0 + lax.broadcasted_iota(jnp.int32, (BQ, 1), 0)
    sq = seg_of(rows, b1, b2, b3)

    key_lanes = lax.broadcasted_iota(jnp.int32, (BK, 2 * HEAD), 1) < HEAD

    def tile(j, carry, masked):
        m, acc = carry
        kv = kv_ref[j, :, :2 * HEAD]
        s = lax.dot_general(q, kv[:, :HEAD], (((1,), (1,)), ((), ())), preferred_element_type=jnp.float32)
        if masked:
            cols = j * BK + lax.broadcasted_iota(jnp.int32, (1, BK), 1)
            s = jnp.where(sq == seg_of(cols, b1, b2, b3), s, -jnp.inf)
        m_new = jnp.maximum(m, jnp.max(s, axis=1, keepdims=True))
        p = jnp.exp(s - m_new)
        alpha = jnp.exp(m - m_new)
        rhs = jnp.where(key_lanes, jnp.ones_like(kv), kv)
        acc = alpha * acc + jnp.dot(p.astype(jnp.bfloat16), rhs, preferred_element_type=jnp.float32)
        return m_new, acc

    def masked_tile(j, carry):
        return tile(j, carry, True)

    def plain_tile(j, carry):
        return tile(j, carry, False)

    m0 = jnp.full((BQ, 1), -1e30, jnp.float32)
    acc0 = jnp.zeros((BQ, 2 * HEAD), jnp.float32)
    carry = lax.fori_loop(lo, mid_lo, masked_tile, (m0, acc0))
    carry = lax.fori_loop(mid_lo, mid_hi, plain_tile, carry)
    _, acc = lax.fori_loop(mid_hi, hi, masked_tile, carry)
    out = jnp.transpose(acc / acc[:, :1])[HEAD:, :].astype(o_ref.dtype)
    per = o_ref.shape[2]
    for b in range(BQ // per):
        o_ref[b] = out[:, b * per:(b + 1) * per]


def attention(mine, counts, tok_rows):
    nk, _, feat = mine.shape
    rows = nk * BK
    nq = rows // BQ
    grid_spec = pltpu.PrefetchScalarGridSpec(
        num_scalar_prefetch=1,
        grid=(nq,),
        in_specs=[
            pl.BlockSpec((1, BQ, feat), lambda i, cnt: (i, 0, 0)),
            pl.BlockSpec((nk, BK, feat), lambda i, cnt: (0, 0, 0)),
        ],
        out_specs=pl.BlockSpec((BQ // tok_rows, HEAD, tok_rows), lambda i, cnt: (i, 0, 0)),
    )
    return pl.pallas_call(
        attn_kernel,
        grid_spec=grid_spec,
        out_shape=jax.ShapeDtypeStruct((rows // tok_rows, HEAD, tok_rows), jnp.bfloat16),
        interpret=INTERPRET,
    )(counts, mine.reshape(nq, BQ, feat), mine)


def shards(tokens, segments, qkv_weight, out_weight, out_bias, ln_gain, ln_bias):
    tok_rows, width = tokens.shape
    groups = lax.axis_size("seq")
    proj_t = jnp.einsum("td,dc->ct", tokens, qkv_weight, preferred_element_type=jnp.float32).astype(jnp.bfloat16)
    grouped = proj_t.reshape(HEADS, 3, HEAD, tok_rows)
    seg_row = jnp.broadcast_to(segments.astype(jnp.bfloat16)[None, None, :], (HEADS, 1, tok_rows))
    payload = jnp.concatenate([grouped[:, 1], grouped[:, 2], grouped[:, 0], seg_row], axis=1)
    mine_t = lax.all_to_all(payload, "seq", split_axis=0, concat_axis=0, tiled=True)
    mine = jnp.swapaxes(mine_t, 1, 2)
    kv_cache = mine[:, :, :2 * HEAD].reshape(groups * tok_rows, 2 * HEAD)
    all_seg = mine_t[:, 3 * HEAD, :].astype(jnp.int32).reshape(groups * tok_rows)
    levels = jnp.arange(SEGS + 1, dtype=jnp.int32)
    counts = jnp.sum((all_seg[None, :] < levels[:, None]).astype(jnp.int32), axis=1)
    context = attention(mine.reshape(groups * tok_rows // BK, BK, 3 * HEAD + 1), counts, tok_rows)
    ctx = lax.all_to_all(context, "seq", split_axis=0, concat_axis=0, tiled=True)
    mixed = (
        jnp.einsum("hct,hcd->td", ctx, out_weight.reshape(HEADS, HEAD, width), preferred_element_type=jnp.float32)
        + out_bias
        + tokens.astype(jnp.float32)
    )
    mean = jnp.mean(mixed, axis=1, keepdims=True)
    centered = mixed - mean
    variance = jnp.mean(centered * centered, axis=1, keepdims=True)
    normed = centered / jnp.sqrt(variance + 1e-05) * ln_gain + ln_bias
    return (normed.astype(jnp.bfloat16), kv_cache)


def solution(mesh):
    in_specs = (P(("rep", "seq"), None), P(("rep", "seq")), P(), P(), P(), P(), P())
    out_specs = (P(("rep", "seq"), None), P("rep", "seq"))
    return jax.shard_map(shards, mesh=mesh, in_specs=in_specs, out_specs=out_specs, check_vma=False)
```

```python
import math

import jax
import jax.numpy as jnp
from jax import lax
from jax.experimental import pallas as pl
from jax.experimental.pallas import tpu as pltpu
from jax.sharding import PartitionSpec as P

HEADS = 16
HEAD = 64
SEGS = 4
BQ = 1024
BK = 512
INTERPRET = False


def seg_of(x, b1, b2, b3):
    return (x >= b1).astype(jnp.int32) + (x >= b2).astype(jnp.int32) + (x >= b3).astype(jnp.int32)


def attn_kernel(cnt_ref, q_ref, kv_ref, o_ref):
    i = pl.program_id(0)
    b1, b2, b3 = cnt_ref[1], cnt_ref[2], cnt_ref[3]
    q0 = i * BQ
    first = seg_of(q0, b1, b2, b3)
    last = seg_of(q0 + BQ - 1, b1, b2, b3)
    start = cnt_ref[first]
    end = cnt_ref[last + 1]
    lo = start // BK
    hi = (end + BK - 1) // BK
    inside = first == last
    mid_lo = jnp.where(inside, (start + BK - 1) // BK, hi)
    mid_hi = jnp.where(inside, jnp.maximum(end // BK, mid_lo), hi)
    scale = 1.0 / math.sqrt(HEAD)
    q = q_ref[0, :, 2 * HEAD:3 * HEAD] * jnp.asarray(scale, jnp.bfloat16)
    rows = q0 + lax.broadcasted_iota(jnp.int32, (BQ, 1), 0)
    sq = seg_of(rows, b1, b2, b3)

    key_lanes = lax.broadcasted_iota(jnp.int32, (BK, 2 * HEAD), 1) < HEAD

    def tile(j, carry, masked):
        m, acc = carry
        kv = kv_ref[j, :, :2 * HEAD]
        s = lax.dot_general(q, kv[:, :HEAD], (((1,), (1,)), ((), ())), preferred_element_type=jnp.float32)
        if masked:
            cols = j * BK + lax.broadcasted_iota(jnp.int32, (1, BK), 1)
            s = jnp.where(sq == seg_of(cols, b1, b2, b3), s, -jnp.inf)
        m_new = jnp.maximum(m, jnp.max(s, axis=1, keepdims=True))
        p = jnp.exp(s - m_new)
        alpha = jnp.exp(m - m_new)
        rhs = jnp.where(key_lanes, jnp.ones_like(kv), kv)
        acc = alpha * acc + jnp.dot(p.astype(jnp.bfloat16), rhs, preferred_element_type=jnp.float32)
        return m_new, acc

    def masked_tile(j, carry):
        return tile(j, carry, True)

    def plain_tile(j, carry):
        return tile(j, carry, False)

    m0 = jnp.full((BQ, 1), -1e30, jnp.float32)
    acc0 = jnp.zeros((BQ, 2 * HEAD), jnp.float32)
    carry = lax.fori_loop(lo, mid_lo, masked_tile, (m0, acc0))
    carry = lax.fori_loop(mid_lo, mid_hi, plain_tile, carry)
    _, acc = lax.fori_loop(mid_hi, hi, masked_tile, carry)
    out = jnp.transpose(acc / acc[:, :1])[HEAD:, :].astype(o_ref.dtype)
    per = o_ref.shape[2]
    for b in range(BQ // per):
        o_ref[b] = out[:, b * per:(b + 1) * per]


def attention(mine, counts, tok_rows):
    nk, _, feat = mine.shape
    rows = nk * BK
    nq = rows // BQ
    grid_spec = pltpu.PrefetchScalarGridSpec(
        num_scalar_prefetch=1,
        grid=(nq,),
        in_specs=[
            pl.BlockSpec((1, BQ, feat), lambda i, cnt: (i, 0, 0)),
            pl.BlockSpec((nk, BK, feat), lambda i, cnt: (0, 0, 0)),
        ],
        out_specs=pl.BlockSpec((BQ // tok_rows, HEAD, tok_rows), lambda i, cnt: (i, 0, 0)),
    )
    return pl.pallas_call(
        attn_kernel,
        grid_spec=grid_spec,
        out_shape=jax.ShapeDtypeStruct((rows // tok_rows, HEAD, tok_rows), jnp.bfloat16),
        interpret=INTERPRET,
    )(counts, mine.reshape(nq, BQ, feat), mine)


def shards(tokens, segments, qkv_weight, out_weight, out_bias, ln_gain, ln_bias):
    tok_rows, width = tokens.shape
    groups = lax.axis_size("seq")
    proj_t = jnp.einsum("td,dc->ct", tokens, qkv_weight, preferred_element_type=jnp.float32).astype(jnp.bfloat16)
    grouped = proj_t.reshape(HEADS, 3, HEAD, tok_rows)
    seg_row = jnp.broadcast_to(segments.astype(jnp.bfloat16)[None, None, :], (HEADS, 1, tok_rows))
    payload = jnp.concatenate([grouped[:, 1], grouped[:, 2], grouped[:, 0], seg_row], axis=1)
    mine_t = lax.all_to_all(payload, "seq", split_axis=0, concat_axis=0, tiled=True)
    mine = jnp.swapaxes(mine_t, 1, 2)
    kv_cache = mine[:, :, :2 * HEAD].reshape(groups * tok_rows, 2 * HEAD)
    all_seg = mine_t[:, 3 * HEAD, :].astype(jnp.int32).reshape(groups * tok_rows)
    levels = jnp.arange(SEGS + 1, dtype=jnp.int32)
    counts = jnp.sum((all_seg[None, :] < levels[:, None]).astype(jnp.int32), axis=1)
    context = attention(mine.reshape(groups * tok_rows // BK, BK, 3 * HEAD + 1), counts, tok_rows)
    ctx = lax.all_to_all(context, "seq", split_axis=0, concat_axis=0, tiled=True)
    mixed = (
        jnp.einsum("hct,hcd->td", ctx, out_weight.reshape(HEADS, HEAD, width), preferred_element_type=jnp.float32)
        + out_bias
        + tokens.astype(jnp.float32)
    )
    mean = jnp.mean(mixed, axis=1, keepdims=True)
    centered = mixed - mean
    variance = jnp.mean(centered * centered, axis=1, keepdims=True)
    normed = centered / jnp.sqrt(variance + 1e-05) * ln_gain + ln_bias
    return (normed.astype(jnp.bfloat16), kv_cache)


def solution(mesh):
    in_specs = (P(("rep", "seq"), None), P(("rep", "seq")), P(), P(), P(), P(), P())
    out_specs = (P(("rep", "seq"), None), P("rep", "seq"))
    return jax.shard_map(shards, mesh=mesh, in_specs=in_specs, out_specs=out_specs, check_vma=False)
```
